256 devices in a mesh: tm: 8 (over x, core), space: 32 (over y, z).
Axes of the slice: x: 4, y: 4, z: 8, core: 2. Of those that a mesh axis runs over, the one named last changes fastest.
Arguments:
- flux: float32 [8, 131072], P('tm', 'space'), may hold values from -6 to 6
- noise: float32 [8, 131072], P('tm', 'space'), may hold values from -6 to 6
- prior_scale: float32 [131072], P('space'), may hold values from 0.3 to 3
- footprints: bfloat16 [8, 1024, 32, 4096], P('tm', 'space'), may hold values from -0.09375 to 0.09375
- soundings: bfloat16 [8, 1024, 32], P('tm', 'space'), may hold values from -6 to 6
- targets: int32 [8, 1024, 1], P('tm', 'space'), may hold values from 0 to 31; in each aligned block of 32 rows (0 to 31, 32 to 63, ..., all dimensions but the last counted through in order) at most 2 rows name the same one
- basis: bfloat16 [131072, 256], P('space'), may hold values from -68 to 68
Outputs:
- proposal: float32 [8, 131072], P('tm', 'space')
- predicted: float32 [8, 1024, 32], P('tm', 'space')
- info_factor: float32 [256, 256], replicated
- whitened_rhs: float32 [256], replicated
The draws below stay inside these ranges and needn't reach their ends.
Inputs may be any that keep to these rules, and one draw needn't show every extreme that they name: `targets`: in the rows of one device no tile is named more than 2 times, and in every draw some device names some tile exactly 2 times.
All inputs are finite; a program needn't handle non-finite values.
Results may differ from the reference program's by a relative error of at most 0.0047.
Values may be sent and summed in bfloat16 or wider, within the bound.
A program may use at most 128 MiB of HBM per device.

```python
import math
import jax
import jax.numpy as jnp
import numpy as np
from jax import lax

PATCH = 64
REACH = 8
RANK = 256
OBS = 32
NB = 32
STEPS = 8
CAP = 2
TILE = 4096
CELLS = 131072
BLOCKS = 1024
OBS_ALL = 262144
N_SPACE = 32


def draw_basis(key, part):
    keys = jax.random.split(key, 3)
    column_scale = jnp.exp(jax.random.uniform(keys[0], (RANK,), jnp.float32) * jnp.log(10.0))
    own_part = jnp.clip(jax.random.normal(keys[1], (CELLS, RANK), jnp.float32), -4.0, 4.0)
    shared_part = jnp.clip(jax.random.normal(keys[2], (CELLS, 16), jnp.float32), -4.0, 4.0)
    mixing = 0.7
    shared_full = jnp.tile(shared_part, (1, RANK // 16))
    return ((own_part + mixing * shared_full) * column_scale[None, :]).astype(jnp.bfloat16)


def block_scale(rng, shape, pieces, least, largest):
    gain = 1.0
    for dim, shards_of in pieces:
        steps = jax.random.uniform(jax.random.fold_in(jax.random.fold_in(rng, 6), dim), (shards_of,), jnp.float32, least / len(pieces), largest / len(pieces))
        gain = gain * jnp.repeat(jnp.exp(steps), shape[dim] // shards_of).reshape((-1,) + (1,) * (len(shape) - 1 - dim))
    return gain


def assign_block(stream_key, own, number, rows, number_of, top, bound, slope):
    sequence = jax.random.permutation(stream_key, number_of)
    heavy_load, ordinary = shares(number_of, rows * top, bound, slope, True), shares(number_of, rows * top, bound, slope, False)
    places = jnp.arange(number_of)

    def named(tallies, rotation):
        used = int((tallies > 0).sum())
        fixed = max(1, used // 4)
        moved = fixed + (places - fixed + rotation * (used - fixed)) % max(1, number_of - fixed)
        return jnp.zeros((number_of,), jnp.int32).at[sequence[jnp.where(places < fixed, places, moved)]].set(jnp.asarray(tallies, jnp.int32))

    tallies = jnp.where(number % 4 == 0, named(heavy_load, number // 4), named(ordinary, number - number // 4 - 1))
    mixed = jax.random.permutation(jax.random.fold_in(own, 3), number_of)
    donor, taker = mixed[0:number_of // 2 * 2:2], mixed[1:number_of // 2 * 2:2]
    room = jnp.minimum(tallies[donor] - 1, bound - tallies[taker]) // 2
    room = jnp.where((donor == sequence[0]) | (taker == sequence[0]) | (tallies[taker] == 0), 0, jnp.maximum(room, 0))
    moved = jax.random.randint(jax.random.fold_in(own, 4), (number_of // 2,), 0, 1 << 20) % (room + 1)
    tallies = tallies.at[donor].add(-moved).at[taker].add(moved)
    items = jnp.searchsorted(jnp.cumsum(tallies), jnp.arange(rows * top), side="right").astype(jnp.int32)
    listing = items.reshape(top, rows).T
    listing = listing[jax.random.permutation(jax.random.fold_in(own, 1), rows)]
    rotation = jax.random.randint(jax.random.fold_in(own, 2), (rows, 1), 0, top)
    return jnp.take_along_axis(listing, (jnp.arange(top)[None, :] + rotation) % top, axis=1)


def shares(count, total, bound, slope, full):
    portions = [(1 << 20) // math.isqrt(rank ** slope) + 1 for rank in range(1, count + 1)]
    largest = bound if full else min(bound, max(-(-total // count), total * portions[0] // sum(portions)))
    least = 1 if total - largest >= count - 1 else 0
    given, rest = [largest] + [least] * (count - 1), total - largest - least * (count - 1)
    while rest > 0:
        candidates = [i for i in range(1, count) if given[i] < largest] or [i for i in range(1, count) if given[i] < bound]
        pool, left = sum([portions[i] for i in candidates]), rest
        for i in candidates:
            extra = min(bound - given[i], max(1, left * portions[i] // pool), rest)
            given[i] = given[i] + extra
            rest = rest - extra
    return np.array(given)


def bell_draw(key, dims, spread, limit, cuts=(), kind=jnp.bfloat16):
    entries = jax.random.normal(key, dims, jnp.float32) * spread
    if len(cuts) > 0:
        entries = block_scale(key, dims, cuts, -0.22, 0.18) * entries
    return jnp.clip(entries, min=-limit, max=limit).astype(kind)


def setup_inputs(seed: int = 0) -> dict:
    arg_keys = jax.random.split(jax.random.key(seed), 8)
    flux = bell_draw(arg_keys[0], (STEPS, CELLS), 1.0, 6.0, ((0, 8), (1, 32)), jnp.float32)
    noise = bell_draw(arg_keys[1], (STEPS, CELLS), 1.0, 6.0, ((0, 8), (1, 32)), jnp.float32)
    prior_scale = jnp.clip(jnp.exp(math.log(3.0) - 2.3025851 * jax.random.uniform(arg_keys[2], (CELLS,), jnp.float32) ** block_scale(arg_keys[2], (CELLS,), ((0, 32),), -0.2, 0.2)), 0.3, 3.0)
    footprints = bell_draw(arg_keys[3], (STEPS, BLOCKS, OBS, TILE), TILE ** -0.5, 0.09375, ((0, 8), (1, 32)))
    soundings = bell_draw(arg_keys[4], (STEPS, BLOCKS, OBS), 1.0, 6.0, ((0, 8), (1, 32)))
    targets_keys = jax.random.split(jax.random.fold_in(arg_keys[5], 1), STEPS * BLOCKS // NB)
    targets_turns = jax.random.permutation(jax.random.fold_in(arg_keys[5], 3), STEPS * BLOCKS // NB)
    targets = jax.vmap(lambda own, number: assign_block(jax.random.fold_in(arg_keys[5], 2), own, number, NB, N_SPACE, 1, CAP, 2))(targets_keys, targets_turns).reshape((STEPS, BLOCKS, 1))
    basis = draw_basis(jax.random.fold_in(arg_keys[7], 71), 0)
    return dict(flux=flux, noise=noise, prior_scale=prior_scale, footprints=footprints, soundings=soundings, targets=targets, basis=basis)


BETA = 0.6
KEEP = 0.8

def kernel_weights(reach):
    offsets = jnp.abs(jnp.arange(-reach, reach + 1).astype(jnp.float32))
    profile = (1.0 + 2.0 * offsets / reach) * jnp.exp(-2.0 * offsets / reach)
    return profile / jnp.sqrt(jnp.sum(profile * profile))

def reference(flux, noise, prior_scale, footprints, soundings, targets, basis):
    weights = kernel_weights(REACH)
    grid_rows = N_SPACE * PATCH
    grid = noise.reshape(STEPS, grid_rows, PATCH)
    padded = jnp.pad(grid, ((0, 0), (REACH, REACH), (0, 0)))
    along_rows = jnp.zeros_like(grid)
    for position in range(2 * REACH + 1):
        along_rows = along_rows + weights[position] * padded[:, position:position + grid_rows, :]
    smooth = jnp.zeros_like(grid)
    for position in range(2 * REACH + 1):
        smooth = smooth + weights[position] * jnp.roll(along_rows, REACH - position, axis=2)
    proposal = KEEP * flux + BETA * prior_scale[None, :] * smooth.reshape(STEPS, CELLS)
    tiles_half = proposal.astype(jnp.bfloat16).reshape(STEPS, N_SPACE, TILE)
    basis_tiles = basis.reshape(N_SPACE, TILE, RANK)
    jac_scale = float(OBS_ALL) ** (-0.5)

    def one_block(carry, block_item):
        gram_sum, projected = carry
        footprint, observed, step_id, target = block_item
        tile_values = tiles_half[step_id, target]
        tile_basis = basis_tiles[target]
        predicted_row = jnp.dot(footprint.astype(jnp.float32), tile_values.astype(jnp.float32), preferred_element_type=jnp.float32)
        jacobian = (jnp.dot(footprint.astype(jnp.float32), tile_basis.astype(jnp.float32), preferred_element_type=jnp.float32) * jac_scale).astype(jnp.bfloat16)
        misfit = observed.astype(jnp.float32) - predicted_row
        gram_sum = gram_sum + jnp.dot(jacobian.T.astype(jnp.float32), jacobian.astype(jnp.float32), preferred_element_type=jnp.float32)
        projected = projected + jnp.dot(jacobian.astype(jnp.float32).T, misfit, precision=lax.Precision.HIGHEST)
        return ((gram_sum, projected), predicted_row)
    step_ids = jnp.broadcast_to(jnp.arange(STEPS, dtype=jnp.int32)[:, None], (STEPS, BLOCKS)).reshape(-1)
    block_items = (footprints.reshape(STEPS * BLOCKS, OBS, TILE), soundings.reshape(STEPS * BLOCKS, OBS), step_ids, targets.reshape(-1).astype(jnp.int32))
    start_carry = (jnp.zeros((RANK, RANK), jnp.float32), jnp.zeros((RANK,), jnp.float32))
    (gram_sum, projected), predicted = lax.scan(one_block, start_carry, block_items)
    information = jnp.eye(RANK, dtype=jnp.float32) + gram_sum
    factor_low = jnp.linalg.cholesky(information)
    whitened_rhs = jax.scipy.linalg.solve_triangular(factor_low, projected, lower=True)
    return (proposal, predicted.reshape(STEPS, BLOCKS, OBS), factor_low.T, whitened_rhs)
```

```python
import jax
import jax.numpy as jnp
from jax import lax
from jax.experimental import pallas as pl
from jax.experimental.pallas import tpu as pltpu
from jax.sharding import PartitionSpec as P

MESH = pl.DeviceIdType.MESH
BLOCKS_HERE = 32
JAC_SCALE = float(262144) ** (-0.5)

PATCH = 64
REACH = 8


BETA = 0.6
KEEP = 0.8


def padded(shard, sides, width):
    for axis, dim in sides:
        devices, length = (lax.axis_size(axis), shard.shape[dim])
        up = [(i, (i + 1) % devices) for i in range(devices - 1)]
        down = [(j, i) for i, j in up]
        last = lax.slice_in_dim(shard, length - width, length, axis=dim)
        leading = lax.slice_in_dim(shard, 0, width, axis=dim)
        before = lax.ppermute(last, axis, up)
        after = lax.ppermute(leading, axis, down)
        shard = jnp.concatenate([before, shard, after], axis=dim)
    return shard


def kernel_weights(reach):
    offsets = jnp.abs(jnp.arange(-reach, reach + 1).astype(jnp.float32))
    profile = (1.0 + 2.0 * offsets / reach) * jnp.exp(-2.0 * offsets / reach)
    return profile / jnp.sqrt(jnp.sum(profile * profile))


def finish_factor(gram_sum, projected):
    information = jnp.eye(gram_sum.shape[0], dtype=jnp.float32) + gram_sum
    factor_low = jnp.linalg.cholesky(information)
    rhs_value = jax.scipy.linalg.solve_triangular(factor_low, projected, lower=True)
    return (factor_low.T, rhs_value)


PA, PB, QA, QB = 368, 816, 560, 560
RX = 448
LAG1, LAG2 = 2, 4


def gather_kernel(tab_ref, mis_ref, fp_ref, basis_ref, aug_ref,
                  own_f, sib_f, tiles, jac, jac_out, tab_v, tab_own, tab_sib,
                  load_sem, pair_send, pair_recv, tree_recv, cross_recv, tree_send, cross_send,
                  jac_send, jac_recv):
    t = lax.axis_index("tm")
    s = lax.axis_index("space")
    x, c = lax.div(t, 2), lax.rem(t, 2)
    y, z = lax.div(s, 8), lax.rem(s, 8)
    sibling = (x * 2 + (1 - c), s)
    z_up = (t, y * 8 + lax.rem(z + 1, 8))
    z_down = (t, y * 8 + lax.rem(z + 7, 8))
    y_up = (t, lax.rem(y + 1, 4) * 8 + z)
    y_down = (t, lax.rem(y + 3, 4) * 8 + z)
    x_up = (lax.rem(x + 1, 4) * 2 + c, s)
    x_down = (lax.rem(x + 3, 4) * 2 + c, s)
    count = BLOCKS_HERE

    own_load = pltpu.make_async_copy(
        basis_ref.at[:, pl.ds(pl.multiple_of(c * 128, 128), 128)], tiles.at[s], load_sem.at[0])
    own_load.start()
    fp_load = pltpu.make_async_copy(fp_ref.at[0], own_f.at[pl.ds(0, count)], load_sem.at[1])
    fp_load.start()
    tab_load = pltpu.make_async_copy(tab_ref, tab_own, load_sem.at[2])
    tab_load.start()

    barrier = pltpu.get_barrier_semaphore()
    for other in (sibling, z_up, z_down, y_up, y_down, x_up, x_down):
        pl.semaphore_signal(barrier, inc=1, device_id=other, device_id_type=MESH)
    pl.semaphore_wait(barrier, 7)

    tab_swap = pltpu.make_async_remote_copy(
        src_ref=tab_ref, dst_ref=tab_v, send_sem=pair_send.at[0], recv_sem=pair_recv.at[0],
        device_id=sibling, device_id_type=MESH)
    tab_swap.start()
    own_load.wait()

    def send(rows, tile, send_sem, recv_sem, device):
        region = tiles.at[tile, rows]
        return pltpu.make_async_remote_copy(
            src_ref=region, dst_ref=region, send_sem=send_sem, recv_sem=recv_sem,
            device_id=device, device_id_type=MESH)

    classes = []
    start = 0
    for size, along_z_first, long_up in ((PA, True, True), (PB, True, False), (QA, False, True), (QB, False, False)):
        classes.append((pl.ds(start, size), along_z_first, long_up, False))
        start += size
    shared_base = start
    if RX:
        classes.append((pl.ds(pl.multiple_of(shared_base + x * RX, 16), RX), True, True, True))
    half = RX // 2

    def piece(owner, first, size):
        return pl.ds(pl.multiple_of(shared_base + owner * RX + first, 16), size)

    def tile_of(n):
        col, i = lax.div(n, 8), lax.rem(n, 8)
        dy = col + lax.div(col, 2) * (1 - 2 * lax.rem(col, 2))
        dz = lax.rem(lax.div(i + 1, 2) * (2 * lax.rem(i, 2) - 1) + 8, 8)
        tile = lax.rem(y - dy + 4, 4) * 8 + lax.rem(z - dz + 8, 8)
        return tile, dy, dz

    def forward(n):
        tile, dy, dz = tile_of(n)
        for k, (rows, along_z_first, long_up, shared) in enumerate(classes):
            hi_z, hi_y = (4, 2) if long_up else (3, 1)

            @pl.when(n > 0)
            def _():
                send(rows, tile, tree_send.at[k], tree_recv.at[k, tile], sibling).wait_recv()

            go_zu = jnp.logical_or(dz == 0, jnp.logical_and(dz >= 1, dz < hi_z))
            go_zd = jnp.logical_or(dz == 0, dz > hi_z + 1)
            go_yu = jnp.logical_or(dy == 0, jnp.logical_and(dy >= 1, dy < hi_y))
            go_yd = jnp.logical_or(dy == 0, dy > hi_y + 1)
            if along_z_first:
                go_zu, go_zd = jnp.logical_and(go_zu, dy == 0), jnp.logical_and(go_zd, dy == 0)
            else:
                go_yu, go_yd = jnp.logical_and(go_yu, dz == 0), jnp.logical_and(go_yd, dz == 0)
            for go, device in ((go_zu, z_up), (go_zd, z_down), (go_yu, y_up), (go_yd, y_down)):
                @pl.when(go)
                def _():
                    send(rows, tile, tree_send.at[k], tree_recv.at[k, tile], device).start()
            if shared:
                @pl.when(n > 0)
                def _():
                    send(rows, tile, cross_send.at[0], cross_recv.at[0, tile], x_up).start()
                    send(rows, tile, cross_send.at[1], cross_recv.at[1, tile], x_down).start()

    def pass_on(n):
        tile, _, _ = tile_of(n)
        below, above = lax.rem(x + 3, 4), lax.rem(x + 1, 4)
        send(piece(below, 0, RX), tile, cross_send.at[0], cross_recv.at[0, tile], sibling).wait_recv()
        send(piece(below, 0, half), tile, cross_send.at[2], cross_recv.at[2, tile], x_up).start()
        send(piece(above, 0, RX), tile, cross_send.at[1], cross_recv.at[1, tile], sibling).wait_recv()
        send(piece(above, half, half), tile, cross_send.at[3], cross_recv.at[3, tile], x_down).start()

    def multiply(n):
        tile, _, _ = tile_of(n)
        if RX:
            far = lax.rem(x + 2, 4)

            @pl.when(n > 0)
            def _():
                send(piece(far, 0, half), tile, cross_send.at[2], cross_recv.at[2, tile], sibling).wait_recv()
                send(piece(far, half, half), tile, cross_send.at[3], cross_recv.at[3, tile], sibling).wait_recv()
        own_a, own_b = tab_own[0, tile * 2], tab_own[0, tile * 2 + 1]
        sib_a, sib_b = tab_sib[0, tile * 2], tab_sib[0, tile * 2 + 1]
        total = jnp.zeros((128, 128), jnp.float32)
        for k in range(4096 // 512):
            ks = pl.ds(k * 512, 512)
            lhs = jnp.concatenate(
                [own_f[own_a, :, ks], own_f[own_b, :, ks], sib_f[sib_a, :, ks], sib_f[sib_b, :, ks]], axis=0)
            total += jnp.dot(lhs, tiles[tile, ks, :], preferred_element_type=jnp.float32)
        total = (total * JAC_SCALE).astype(jnp.bfloat16)
        rows = pl.ds(pl.multiple_of(tile * 64, 64), 64)
        jac[c, rows, :] = total[:64]
        jac_out[rows, :] = total[64:]
        pltpu.make_async_remote_copy(
            src_ref=jac_out.at[rows], dst_ref=jac.at[c, rows], send_sem=jac_send, recv_sem=jac_recv,
            device_id=sibling, device_id_type=MESH).start()

    forward(0)
    fp_swap = pltpu.make_async_remote_copy(
        src_ref=fp_ref.at[0], dst_ref=sib_f.at[pl.ds(0, count)], send_sem=pair_send.at[1],
        recv_sem=pair_recv.at[1], device_id=sibling, device_id_type=MESH)
    fp_swap.start()
    own_f[count] = jnp.zeros(own_f.shape[1:], own_f.dtype)
    sib_f[count] = jnp.zeros(sib_f.shape[1:], sib_f.dtype)
    tab_swap.wait()
    sib_load = pltpu.make_async_copy(tab_v, tab_sib, load_sem.at[3])
    sib_load.start()
    tab_load.wait()
    sib_load.wait()
    fp_load.wait()
    fp_swap.wait()

    def step(n, carry):
        @pl.when(n < 32)
        def _():
            forward(n)
        if RX:
            @pl.when(jnp.logical_and(n >= LAG1 + 1, n < 32 + LAG1))
            def _():
                pass_on(n - LAG1)
        lag = LAG2 if RX else 0

        @pl.when(n >= lag)
        def _():
            multiply(n - lag)
        return carry

    if RX:
        lax.fori_loop(1, 32 + LAG2, step, 0)
    else:
        multiply(jnp.int32(0))
        lax.fori_loop(1, 32, step, 0)

    for k, (rows, _, _, _) in enumerate(classes):
        region = tiles.at[pl.ds(0, 31), rows]
        pltpu.make_async_copy(region, region, tree_send.at[k]).wait()
    if RX:
        for k, size in enumerate((RX, RX, half, half)):
            region = tiles.at[pl.ds(0, 31), pl.ds(0, size)]
            pltpu.make_async_copy(region, region, cross_send.at[k]).wait()
    whole = pltpu.make_async_remote_copy(
        src_ref=jac_out, dst_ref=jac.at[1 - c], send_sem=jac_send, recv_sem=jac_recv,
        device_id=sibling, device_id_type=MESH)
    whole.wait()
    low, high = jac[0], jac[1]

    def gram(a, b):
        return lax.dot_general(a, b, (((0,), (0,)), ((), ())), preferred_element_type=jnp.float32)

    aug_ref[0:128, :] = gram(low, low)
    aug_ref[128:256, :] = gram(low, high)
    aug_ref[256:384, :] = gram(high, high)
    mis = mis_ref[...]
    mis_a = mis.astype(jnp.bfloat16)
    rest = mis - mis_a.astype(jnp.float32)
    mis_b = rest.astype(jnp.bfloat16)
    mis_c = (rest - mis_b.astype(jnp.float32)).astype(jnp.bfloat16)
    aug_ref[384:, :] = jnp.zeros((128, 128), jnp.float32)
    for k, side in enumerate((low, high)):
        part = sum(jnp.dot(m, side, preferred_element_type=jnp.float32) for m in (mis_c, mis_b, mis_a))
        aug_ref[384 + 8 * k:392 + 8 * k, :] = part


def gathered_information(table, misfit, footprints, basis):
    vm = pl.BlockSpec(memory_space=pltpu.VMEM)
    hbm = pl.BlockSpec(memory_space=pl.ANY)
    dma = pltpu.SemaphoreType.DMA
    return pl.pallas_call(
        gather_kernel,
        out_shape=jax.ShapeDtypeStruct((512, 128), jnp.float32),
        in_specs=[vm, vm, hbm, hbm],
        out_specs=vm,
        scratch_shapes=[
            pltpu.VMEM((33, 32, 4096), jnp.bfloat16),
            pltpu.VMEM((33, 32, 4096), jnp.bfloat16),
            pltpu.VMEM((32, 4096, 128), jnp.bfloat16),
            pltpu.VMEM((2, 2048, 128), jnp.bfloat16),
            pltpu.VMEM((2048, 128), jnp.bfloat16),
            pltpu.VMEM((1, 128), jnp.int32),
            pltpu.SMEM((1, 128), jnp.int32),
            pltpu.SMEM((1, 128), jnp.int32),
            dma((4,)), dma((2,)), dma((2,)), dma((5, 32)), dma((4, 32)), dma((5,)), dma((4,)),
            dma, dma,
        ],
        compiler_params=pltpu.CompilerParams(
            collective_id=0, has_side_effects=True, vmem_limit_bytes=60 * 1024 * 1024),
        name="gather_information",
    )(table, misfit, footprints, basis)


def per_device(flux, noise, prior_scale, footprints, soundings, targets, basis):
    block_count = footprints.shape[1]
    obs_count = footprints.shape[2]
    cell_count = footprints.shape[3]
    patch_edge = PATCH
    tile_count = 32
    weights = kernel_weights(REACH)
    extended = padded(noise, (("space", 1),), REACH * patch_edge)
    extended_grid = extended.reshape(patch_edge + 2 * REACH, patch_edge)
    row_offset = jnp.arange(patch_edge + 2 * REACH)[None, :] - jnp.arange(patch_edge)[:, None]
    col_offset = (
        jnp.arange(patch_edge)[:, None] - jnp.arange(patch_edge)[None, :] + REACH
    ) % patch_edge
    row_band = jnp.zeros((patch_edge, patch_edge + 2 * REACH), jnp.float32)
    col_circulant = jnp.zeros((patch_edge, patch_edge), jnp.float32)
    for position in range(2 * REACH + 1):
        row_band = row_band + weights[position] * (row_offset == position).astype(jnp.float32)
        col_circulant = col_circulant + weights[position] * (col_offset == position).astype(
            jnp.float32
        )
    along_rows = jnp.dot(row_band, extended_grid, precision=lax.Precision.HIGHEST)
    smooth = jnp.dot(along_rows, col_circulant, precision=lax.Precision.HIGHEST)
    proposal = KEEP * flux + BETA * prior_scale[None, :] * smooth.reshape(1, cell_count)
    destination = targets[0, :, 0]
    dest_onehot = destination[:, None] == jnp.arange(tile_count)[None, :]
    counts = dest_onehot.astype(jnp.int32)
    slot_rank = jnp.sum((jnp.cumsum(counts, axis=0) - counts) * counts, axis=1)
    slot_of = destination * 2 + slot_rank
    slot_match = slot_of[None, :] == jnp.arange(2 * tile_count)[:, None]
    source_of = jnp.sum(jnp.where(slot_match, jnp.arange(block_count)[None, :] + 1, 0), axis=1) - 1
    source_of = jnp.where(source_of < 0, block_count, source_of)
    table = jnp.zeros((1, 128), jnp.int32).at[0, : 2 * tile_count].set(source_of)
    all_half = lax.all_gather(proposal[0].astype(jnp.bfloat16), "space")
    every = jnp.dot(
        footprints[0].reshape(block_count * obs_count, cell_count), all_half.T,
        preferred_element_type=jnp.float32,
    ).reshape(block_count, obs_count, tile_count)
    predicted = jnp.sum(jnp.where(dest_onehot[:, None, :], every, 0.0), axis=2)
    misfit = soundings[0].astype(jnp.float32) - predicted
    misfit_slots = jnp.sum(jnp.where(slot_match[:, :, None], misfit[None], 0.0), axis=1)
    misfit_rows = jnp.zeros((8, 2048), jnp.float32).at[0].set(misfit_slots.reshape(-1))
    aug = gathered_information(table, misfit_rows, footprints, basis)
    aug = lax.psum(aug, ("tm", "space"))
    cross = aug[128:256]
    gram = jnp.block([[aug[0:128], cross], [cross.T, aug[256:384]]])
    projected = jnp.concatenate([aug[384], aug[392]])
    factor_up, rhs_value = finish_factor(gram, projected)
    return (proposal, predicted[None], factor_up, rhs_value)


def solution(mesh):
    return jax.shard_map(
        per_device,
        mesh=mesh,
        in_specs=(
            P("tm", "space"),
            P("tm", "space"),
            P("space"),
            P("tm", "space", None, None),
            P("tm", "space", None),
            P("tm", "space", None),
            P("space", None),
        ),
        out_specs=(P("tm", "space"), P("tm", "space", None), P(), P()),
        check_vma=False,
    )
```

```python
import jax
import jax.numpy as jnp
from jax import lax
from jax.experimental import pallas as pl
from jax.experimental.pallas import tpu as pltpu
from jax.sharding import PartitionSpec as P

MESH = pl.DeviceIdType.MESH
HIGHEST = lax.Precision.HIGHEST
BLOCKS_HERE = 32
JAC_SCALE = float(262144) ** (-0.5)

PATCH = 64
REACH = 8


BETA = 0.6
KEEP = 0.8


def padded(shard, sides, width):
    for axis, dim in sides:
        devices, length = (lax.axis_size(axis), shard.shape[dim])
        up = [(i, (i + 1) % devices) for i in range(devices - 1)]
        down = [(j, i) for i, j in up]
        last = lax.slice_in_dim(shard, length - width, length, axis=dim)
        leading = lax.slice_in_dim(shard, 0, width, axis=dim)
        before = lax.ppermute(last, axis, up)
        after = lax.ppermute(leading, axis, down)
        shard = jnp.concatenate([before, shard, after], axis=dim)
    return shard


def kernel_weights(reach):
    offsets = jnp.abs(jnp.arange(-reach, reach + 1).astype(jnp.float32))
    profile = (1.0 + 2.0 * offsets / reach) * jnp.exp(-2.0 * offsets / reach)
    return profile / jnp.sqrt(jnp.sum(profile * profile))


PA, PB, QA, QB = 368, 816, 560, 560
RX = 448
LAG1, LAG2 = 2, 4


def gather_kernel(tab_ref, mis_ref, fp_ref, basis_ref, aug_ref,
                  own_f, sib_f, tiles, jac, jac_out, tab_v, tab_own, tab_sib,
                  load_sem, pair_send, pair_recv, tree_recv, cross_recv, tree_send, cross_send,
                  jac_send, jac_recv):
    t = lax.axis_index("tm")
    s = lax.axis_index("space")
    x, c = lax.div(t, 2), lax.rem(t, 2)
    y, z = lax.div(s, 8), lax.rem(s, 8)
    sibling = (x * 2 + (1 - c), s)
    z_up = (t, y * 8 + lax.rem(z + 1, 8))
    z_down = (t, y * 8 + lax.rem(z + 7, 8))
    y_up = (t, lax.rem(y + 1, 4) * 8 + z)
    y_down = (t, lax.rem(y + 3, 4) * 8 + z)
    x_up = (lax.rem(x + 1, 4) * 2 + c, s)
    x_down = (lax.rem(x + 3, 4) * 2 + c, s)
    count = BLOCKS_HERE

    own_load = pltpu.make_async_copy(
        basis_ref.at[:, pl.ds(pl.multiple_of(c * 128, 128), 128)], tiles.at[s], load_sem.at[0])
    own_load.start()
    fp_load = pltpu.make_async_copy(fp_ref.at[0], own_f.at[pl.ds(0, count)], load_sem.at[1])
    fp_load.start()
    tab_load = pltpu.make_async_copy(tab_ref, tab_own, load_sem.at[2])
    tab_load.start()

    barrier = pltpu.get_barrier_semaphore()
    for other in (sibling, z_up, z_down, y_up, y_down, x_up, x_down):
        pl.semaphore_signal(barrier, inc=1, device_id=other, device_id_type=MESH)
    pl.semaphore_wait(barrier, 7)

    tab_swap = pltpu.make_async_remote_copy(
        src_ref=tab_ref, dst_ref=tab_v, send_sem=pair_send.at[0], recv_sem=pair_recv.at[0],
        device_id=sibling, device_id_type=MESH)
    tab_swap.start()
    own_load.wait()

    def send(rows, tile, send_sem, recv_sem, device):
        region = tiles.at[tile, rows]
        return pltpu.make_async_remote_copy(
            src_ref=region, dst_ref=region, send_sem=send_sem, recv_sem=recv_sem,
            device_id=device, device_id_type=MESH)

    classes = []
    start = 0
    for size, along_z_first, long_up in ((PA, True, True), (PB, True, False), (QA, False, True), (QB, False, False)):
        classes.append((pl.ds(start, size), along_z_first, long_up, False))
        start += size
    shared_base = start
    if RX:
        classes.append((pl.ds(pl.multiple_of(shared_base + x * RX, 16), RX), True, True, True))
    half = RX // 2

    def piece(owner, first, size):
        return pl.ds(pl.multiple_of(shared_base + owner * RX + first, 16), size)

    def tile_of(n):
        col, i = lax.div(n, 8), lax.rem(n, 8)
        dy = col + lax.div(col, 2) * (1 - 2 * lax.rem(col, 2))
        dz = lax.rem(lax.div(i + 1, 2) * (2 * lax.rem(i, 2) - 1) + 8, 8)
        tile = lax.rem(y - dy + 4, 4) * 8 + lax.rem(z - dz + 8, 8)
        return tile, dy, dz

    def forward(n):
        tile, dy, dz = tile_of(n)
        for k, (rows, along_z_first, long_up, shared) in enumerate(classes):
            hi_z, hi_y = (4, 2) if long_up else (3, 1)

            @pl.when(n > 0)
            def _():
                send(rows, tile, tree_send.at[k], tree_recv.at[k, tile], sibling).wait_recv()

            go_zu = jnp.logical_or(dz == 0, jnp.logical_and(dz >= 1, dz < hi_z))
            go_zd = jnp.logical_or(dz == 0, dz > hi_z + 1)
            go_yu = jnp.logical_or(dy == 0, jnp.logical_and(dy >= 1, dy < hi_y))
            go_yd = jnp.logical_or(dy == 0, dy > hi_y + 1)
            if along_z_first:
                go_zu, go_zd = jnp.logical_and(go_zu, dy == 0), jnp.logical_and(go_zd, dy == 0)
            else:
                go_yu, go_yd = jnp.logical_and(go_yu, dz == 0), jnp.logical_and(go_yd, dz == 0)
            for go, device in ((go_zu, z_up), (go_zd, z_down), (go_yu, y_up), (go_yd, y_down)):
                @pl.when(go)
                def _():
                    send(rows, tile, tree_send.at[k], tree_recv.at[k, tile], device).start()
            if shared:
                @pl.when(n > 0)
                def _():
                    send(rows, tile, cross_send.at[0], cross_recv.at[0, tile], x_up).start()
                    send(rows, tile, cross_send.at[1], cross_recv.at[1, tile], x_down).start()

    def pass_on(n):
        tile, _, _ = tile_of(n)
        below, above = lax.rem(x + 3, 4), lax.rem(x + 1, 4)
        send(piece(below, 0, RX), tile, cross_send.at[0], cross_recv.at[0, tile], sibling).wait_recv()
        send(piece(below, 0, half), tile, cross_send.at[2], cross_recv.at[2, tile], x_up).start()
        send(piece(above, 0, RX), tile, cross_send.at[1], cross_recv.at[1, tile], sibling).wait_recv()
        send(piece(above, half, half), tile, cross_send.at[3], cross_recv.at[3, tile], x_down).start()

    def multiply(n):
        tile, _, _ = tile_of(n)
        if RX:
            far = lax.rem(x + 2, 4)

            @pl.when(n > 0)
            def _():
                send(piece(far, 0, half), tile, cross_send.at[2], cross_recv.at[2, tile], sibling).wait_recv()
                send(piece(far, half, half), tile, cross_send.at[3], cross_recv.at[3, tile], sibling).wait_recv()
        own_a, own_b = tab_own[0, tile * 2], tab_own[0, tile * 2 + 1]
        sib_a, sib_b = tab_sib[0, tile * 2], tab_sib[0, tile * 2 + 1]
        total = jnp.zeros((128, 128), jnp.float32)
        for k in range(4096 // 512):
            ks = pl.ds(k * 512, 512)
            lhs = jnp.concatenate(
                [own_f[own_a, :, ks], own_f[own_b, :, ks], sib_f[sib_a, :, ks], sib_f[sib_b, :, ks]], axis=0)
            total += jnp.dot(lhs, tiles[tile, ks, :], preferred_element_type=jnp.float32)
        total = (total * JAC_SCALE).astype(jnp.bfloat16)
        rows = pl.ds(pl.multiple_of(tile * 64, 64), 64)
        jac[c, rows, :] = total[:64]
        jac_out[rows, :] = total[64:]
        pltpu.make_async_remote_copy(
            src_ref=jac_out.at[rows], dst_ref=jac.at[c, rows], send_sem=jac_send, recv_sem=jac_recv,
            device_id=sibling, device_id_type=MESH).start()

    forward(0)
    fp_swap = pltpu.make_async_remote_copy(
        src_ref=fp_ref.at[0], dst_ref=sib_f.at[pl.ds(0, count)], send_sem=pair_send.at[1],
        recv_sem=pair_recv.at[1], device_id=sibling, device_id_type=MESH)
    fp_swap.start()
    own_f[count] = jnp.zeros(own_f.shape[1:], own_f.dtype)
    sib_f[count] = jnp.zeros(sib_f.shape[1:], sib_f.dtype)
    tab_swap.wait()
    sib_load = pltpu.make_async_copy(tab_v, tab_sib, load_sem.at[3])
    sib_load.start()
    tab_load.wait()
    sib_load.wait()
    fp_load.wait()
    fp_swap.wait()

    def step(n, carry):
        @pl.when(n < 32)
        def _():
            forward(n)
        if RX:
            @pl.when(jnp.logical_and(n >= LAG1 + 1, n < 32 + LAG1))
            def _():
                pass_on(n - LAG1)
        lag = LAG2 if RX else 0

        @pl.when(n >= lag)
        def _():
            multiply(n - lag)
        return carry

    if RX:
        lax.fori_loop(1, 32 + LAG2, step, 0)
    else:
        multiply(jnp.int32(0))
        lax.fori_loop(1, 32, step, 0)

    for k, (rows, _, _, _) in enumerate(classes):
        region = tiles.at[pl.ds(0, 31), rows]
        pltpu.make_async_copy(region, region, tree_send.at[k]).wait()
    if RX:
        for k, size in enumerate((RX, RX, half, half)):
            region = tiles.at[pl.ds(0, 31), pl.ds(0, size)]
            pltpu.make_async_copy(region, region, cross_send.at[k]).wait()
    whole = pltpu.make_async_remote_copy(
        src_ref=jac_out, dst_ref=jac.at[1 - c], send_sem=jac_send, recv_sem=jac_recv,
        device_id=sibling, device_id_type=MESH)
    whole.wait()
    low, high = jac[0], jac[1]

    def gram(a, b):
        return lax.dot_general(a, b, (((0,), (0,)), ((), ())), preferred_element_type=jnp.float32)

    aug_ref[0:128, :] = gram(low, low)
    aug_ref[128:256, :] = gram(low, high)
    aug_ref[256:384, :] = gram(high, high)
    mis = mis_ref[...]
    mis_a = mis.astype(jnp.bfloat16)
    rest = mis - mis_a.astype(jnp.float32)
    mis_b = rest.astype(jnp.bfloat16)
    mis_c = (rest - mis_b.astype(jnp.float32)).astype(jnp.bfloat16)
    aug_ref[384:, :] = jnp.zeros((128, 128), jnp.float32)
    for k, side in enumerate((low, high)):
        part = sum(jnp.dot(m, side, preferred_element_type=jnp.float32) for m in (mis_c, mis_b, mis_a))
        aug_ref[384 + 8 * k:392 + 8 * k, :] = part


def gathered_information(table, misfit, footprints, basis):
    vm = pl.BlockSpec(memory_space=pltpu.VMEM)
    hbm = pl.BlockSpec(memory_space=pl.ANY)
    dma = pltpu.SemaphoreType.DMA
    return pl.pallas_call(
        gather_kernel,
        out_shape=jax.ShapeDtypeStruct((512, 128), jnp.float32),
        in_specs=[vm, vm, hbm, hbm],
        out_specs=vm,
        scratch_shapes=[
            pltpu.VMEM((33, 32, 4096), jnp.bfloat16),
            pltpu.VMEM((33, 32, 4096), jnp.bfloat16),
            pltpu.VMEM((32, 4096, 128), jnp.bfloat16),
            pltpu.VMEM((2, 2048, 128), jnp.bfloat16),
            pltpu.VMEM((2048, 128), jnp.bfloat16),
            pltpu.VMEM((1, 128), jnp.int32),
            pltpu.SMEM((1, 128), jnp.int32),
            pltpu.SMEM((1, 128), jnp.int32),
            dma((4,)), dma((2,)), dma((2,)), dma((5, 32)), dma((4, 32)), dma((5,)), dma((4,)),
            dma, dma,
        ],
        compiler_params=pltpu.CompilerParams(
            collective_id=0, has_side_effects=True, vmem_limit_bytes=60 * 1024 * 1024),
        name="gather_information",
    )(table, misfit, footprints, basis)


def factor_rows(work, out_u, out_v):
    row = lax.broadcasted_iota(jnp.int32, (32, 128), 0)
    lane = lax.broadcasted_iota(jnp.int32, (32, 128), 1)
    wide_row = lax.broadcasted_iota(jnp.int32, (32, 256), 0)
    wide_lane = lax.broadcasted_iota(jnp.int32, (32, 256), 1)
    for k in range(8):
        k0, c0 = 32 * k, 128 * (k // 4)
        off = k0 - c0
        eye0 = (off + 64) % 128
        rows = work[k0:k0 + 32, :]
        e = jnp.where(jnp.logical_and(lane >= off, lane < off + 32), rows[:, c0:c0 + 128], 0.0)
        e = e + (lane - eye0 == row).astype(jnp.float32)
        for j in range(32):
            column = jnp.where(row > j, jnp.broadcast_to(e[:, off + j:off + j + 1], (32, 128)), 0.0)
            pivot = e[j:j + 1, off + j:off + j + 1]
            e = e - column * (e[j:j + 1, :] * (1.0 / pivot))
        diagonal = jnp.sum(jnp.where(lane == row + off, e, 0.0), axis=1, keepdims=True)
        e = e * lax.rsqrt(diagonal)
        inverse = e[:, eye0:eye0 + 32]
        panel = jnp.dot(inverse, rows[:, c0:], preferred_element_type=jnp.float32, precision=HIGHEST)
        upper = panel[:, :256 - c0]
        if c0:
            upper = jnp.concatenate([jnp.zeros((32, c0), jnp.float32), upper], axis=1)
        upper = jnp.where(wide_lane >= wide_row + k0, upper, 0.0)
        out_u[k0:k0 + 32, :] = upper
        out_v[k0:k0 + 32, :] = panel[:, 256 - c0:]
        if k < 7:
            k1 = k0 + 32
            c1 = 128 * (k1 // 128)
            left = panel[:, c1 - c0:256 - c0]
            update = lax.dot_general(left, panel[:, c1 - c0:], (((0,), (0,)), ((), ())),
                                     preferred_element_type=jnp.float32, precision=HIGHEST)
            work[k1:, c1:] = work[k1:, c1:] - update[k1 - c1:]


def finish_kernel(aug_ref, u_ref, v_ref, parts, sums, full, work,
                  send_a, recv_a, send_b, recv_b, send_c, recv_c):
    t = lax.axis_index("tm")
    s = lax.axis_index("space")
    x, c = lax.div(t, 2), lax.rem(t, 2)
    y, z = lax.div(s, 8), lax.rem(s, 8)
    a = c * 8 + z
    b = x * 4 + y

    def in_a(k):
        other = lax.rem(a + k, 16)
        return other, (x * 2 + lax.div(other, 8), y * 8 + lax.rem(other, 8))

    def in_b(k):
        other = lax.rem(b + k, 16)
        return other, (lax.div(other, 4) * 2 + c, lax.rem(other, 4) * 8 + z)

    barrier = pltpu.get_barrier_semaphore()

    def greet(k, carry):
        for group in (in_a, in_b):
            pl.semaphore_signal(barrier, inc=1, device_id=group(k)[1], device_id_type=MESH)
        return carry

    lax.fori_loop(1, 16, greet, 0)
    pl.semaphore_wait(barrier, 30)

    def rows(index):
        return pl.ds(pl.multiple_of(index * 32, 32), 32)

    def scatter(k, carry):
        other, device = in_a(k)
        pltpu.make_async_remote_copy(
            src_ref=aug_ref.at[rows(other)], dst_ref=parts.at[k - 1], send_sem=send_a, recv_sem=recv_a,
            device_id=device, device_id_type=MESH).start()
        return carry

    lax.fori_loop(1, 16, scatter, 0)

    def settle(region, send_sem, recv_sem):
        pltpu.make_async_copy(region, region, send_sem).wait()
        pltpu.make_async_copy(region, region, recv_sem).wait()

    settle(parts, send_a, recv_a)
    own = aug_ref[rows(a), :]
    for k in range(15):
        own = own + parts[k]
    sums[b] = own

    def exchange(k, carry):
        _, device = in_b(k)
        pltpu.make_async_remote_copy(
            src_ref=sums.at[b], dst_ref=sums.at[b], send_sem=send_b, recv_sem=recv_b,
            device_id=device, device_id_type=MESH).start()
        return carry

    lax.fori_loop(1, 16, exchange, 0)
    settle(parts, send_b, recv_b)
    total = sums[0]
    for k in range(1, 16):
        total = total + sums[k]
    full[rows(a), :] = total

    def spread(k, carry):
        _, device = in_a(k)
        pltpu.make_async_remote_copy(
            src_ref=full.at[rows(a)], dst_ref=full.at[rows(a)], send_sem=send_c, recv_sem=recv_c,
            device_id=device, device_id_type=MESH).start()
        return carry

    lax.fori_loop(1, 16, spread, 0)
    settle(parts, send_c, recv_c)
    square = (128, 128)
    eye = (lax.broadcasted_iota(jnp.int32, square, 0) == lax.broadcasted_iota(jnp.int32, square, 1))
    eye = eye.astype(jnp.float32)
    rhs = full[384:512, :].T
    work[0:128, 0:128] = full[0:128, :] + eye
    work[0:128, 128:256] = full[128:256, :]
    work[128:256, 128:256] = full[256:384, :] + eye
    work[0:128, 256:384] = rhs
    work[128:256, 256:384] = jnp.concatenate([rhs[:, 8:], rhs[:, :8]], axis=1)
    factor_rows(work, u_ref, v_ref)


def finished(aug):
    vm = pl.BlockSpec(memory_space=pltpu.VMEM)
    dma = pltpu.SemaphoreType.DMA
    upper, rhs = pl.pallas_call(
        finish_kernel,
        out_shape=(jax.ShapeDtypeStruct((256, 256), jnp.float32), jax.ShapeDtypeStruct((256, 128), jnp.float32)),
        in_specs=[vm],
        out_specs=(vm, vm),
        scratch_shapes=[
            pltpu.VMEM((15, 32, 128), jnp.float32),
            pltpu.VMEM((16, 32, 128), jnp.float32),
            pltpu.VMEM((512, 128), jnp.float32),
            pltpu.VMEM((256, 384), jnp.float32),
            dma, dma, dma, dma, dma, dma,
        ],
        compiler_params=pltpu.CompilerParams(collective_id=1, has_side_effects=True),
        name="sum_and_factor",
    )(aug)
    return upper, rhs[:, 0]


def per_device(flux, noise, prior_scale, footprints, soundings, targets, basis):
    block_count = footprints.shape[1]
    obs_count = footprints.shape[2]
    cell_count = footprints.shape[3]
    patch_edge = PATCH
    tile_count = 32
    weights = kernel_weights(REACH)
    extended = padded(noise, (("space", 1),), REACH * patch_edge)
    extended_grid = extended.reshape(patch_edge + 2 * REACH, patch_edge)
    row_offset = jnp.arange(patch_edge + 2 * REACH)[None, :] - jnp.arange(patch_edge)[:, None]
    col_offset = (
        jnp.arange(patch_edge)[:, None] - jnp.arange(patch_edge)[None, :] + REACH
    ) % patch_edge
    row_band = jnp.zeros((patch_edge, patch_edge + 2 * REACH), jnp.float32)
    col_circulant = jnp.zeros((patch_edge, patch_edge), jnp.float32)
    for position in range(2 * REACH + 1):
        row_band = row_band + weights[position] * (row_offset == position).astype(jnp.float32)
        col_circulant = col_circulant + weights[position] * (col_offset == position).astype(
            jnp.float32
        )
    along_rows = jnp.dot(row_band, extended_grid, precision=lax.Precision.HIGHEST)
    smooth = jnp.dot(along_rows, col_circulant, precision=lax.Precision.HIGHEST)
    proposal = KEEP * flux + BETA * prior_scale[None, :] * smooth.reshape(1, cell_count)
    destination = targets[0, :, 0]
    dest_onehot = destination[:, None] == jnp.arange(tile_count)[None, :]
    counts = dest_onehot.astype(jnp.int32)
    slot_rank = jnp.sum((jnp.cumsum(counts, axis=0) - counts) * counts, axis=1)
    slot_of = destination * 2 + slot_rank
    slot_match = slot_of[None, :] == jnp.arange(2 * tile_count)[:, None]
    source_of = jnp.sum(jnp.where(slot_match, jnp.arange(block_count)[None, :] + 1, 0), axis=1) - 1
    source_of = jnp.where(source_of < 0, block_count, source_of)
    table = jnp.zeros((1, 128), jnp.int32).at[0, : 2 * tile_count].set(source_of)
    all_half = lax.all_gather(proposal[0].astype(jnp.bfloat16), "space")
    every = jnp.dot(
        footprints[0].reshape(block_count * obs_count, cell_count), all_half.T,
        preferred_element_type=jnp.float32,
    ).reshape(block_count, obs_count, tile_count)
    predicted = jnp.sum(jnp.where(dest_onehot[:, None, :], every, 0.0), axis=2)
    misfit = soundings[0].astype(jnp.float32) - predicted
    misfit_slots = jnp.sum(jnp.where(slot_match[:, :, None], misfit[None], 0.0), axis=1)
    misfit_rows = jnp.zeros((8, 2048), jnp.float32).at[0].set(misfit_slots.reshape(-1))
    aug = gathered_information(table, misfit_rows, footprints, basis)
    factor_up, rhs_value = finished(aug)
    return (proposal, predicted[None], factor_up, rhs_value)


def solution(mesh):
    return jax.shard_map(
        per_device,
        mesh=mesh,
        in_specs=(
            P("tm", "space"),
            P("tm", "space"),
            P("space"),
            P("tm", "space", None, None),
            P("tm", "space", None),
            P("tm", "space", None),
            P("space", None),
        ),
        out_specs=(P("tm", "space"), P("tm", "space", None), P(), P()),
        check_vma=False,
    )
```

```python
import math

import jax
import jax.numpy as jnp
from jax import lax
from jax.experimental import pallas as pl
from jax.experimental.pallas import tpu as pltpu
from jax.sharding import PartitionSpec as P

MESH = pl.DeviceIdType.MESH
HIGHEST = lax.Precision.HIGHEST
BLOCKS_HERE = 32
JAC_SCALE = float(262144) ** (-0.5)
REACH = 8
BETA = 0.6
KEEP = 0.8


def kernel_weights(reach):
    profile = [(1.0 + 2.0 * abs(d) / reach) * math.exp(-2.0 * abs(d) / reach) for d in range(-reach, reach + 1)]
    norm = math.sqrt(sum(p * p for p in profile))
    return [p / norm for p in profile]


KERNEL = kernel_weights(REACH)


def factor_rows(work, out_u, out_v):
    row = lax.broadcasted_iota(jnp.int32, (32, 128), 0)
    lane = lax.broadcasted_iota(jnp.int32, (32, 128), 1)
    wide_row = lax.broadcasted_iota(jnp.int32, (32, 256), 0)
    wide_lane = lax.broadcasted_iota(jnp.int32, (32, 256), 1)
    for k in range(8):
        k0, c0 = 32 * k, 128 * (k // 4)
        off = k0 - c0
        eye0 = (off + 64) % 128
        rows = work[k0:k0 + 32, :]
        e = jnp.where(jnp.logical_and(lane >= off, lane < off + 32), rows[:, c0:c0 + 128], 0.0)
        e = e + (lane - eye0 == row).astype(jnp.float32)
        for j in range(32):
            column = jnp.where(row > j, jnp.broadcast_to(e[:, off + j:off + j + 1], (32, 128)), 0.0)
            pivot = e[j:j + 1, off + j:off + j + 1]
            e = e - column * (e[j:j + 1, :] * (1.0 / pivot))
        diagonal = jnp.sum(jnp.where(lane == row + off, e, 0.0), axis=1, keepdims=True)
        e = e * lax.rsqrt(diagonal)
        inverse = e[:, eye0:eye0 + 32]
        panel = jnp.dot(inverse, rows[:, c0:], preferred_element_type=jnp.float32, precision=HIGHEST)
        upper = panel[:, :256 - c0]
        if c0:
            upper = jnp.concatenate([jnp.zeros((32, c0), jnp.float32), upper], axis=1)
        upper = jnp.where(wide_lane >= wide_row + k0, upper, 0.0)
        out_u[k0:k0 + 32, :] = upper
        out_v[k0:k0 + 32, :] = panel[:, 256 - c0:]
        if k < 7:
            k1 = k0 + 32
            c1 = 128 * (k1 // 128)
            left = panel[:, c1 - c0:256 - c0]
            update = lax.dot_general(left, panel[:, c1 - c0:], (((0,), (0,)), ((), ())),
                                     preferred_element_type=jnp.float32, precision=HIGHEST)
            work[k1:, c1:] = work[k1:, c1:] - update[k1 - c1:]


PA, PB, QA, QB = 368, 816, 560, 560
RX = 448
LAG1, LAG2 = 2, 4


def weight(position):
    return KERNEL[REACH + position]


def smoothing_matrices():
    lane = lax.broadcasted_iota(jnp.int32, (128, 128), 1)
    source = lax.broadcasted_iota(jnp.int32, (128, 128), 0)
    same = lax.div(lane, 64) == lax.div(source, 64)
    gap = lax.rem(source - lane + 64 + REACH, 64)
    columns = jnp.zeros((128, 128), jnp.float32)
    for b in range(-REACH, REACH + 1):
        columns = columns + jnp.where(jnp.logical_and(same, gap == b + REACH), weight(b), 0.0)
    row = lax.broadcasted_iota(jnp.int32, (32, 48), 0)
    shift = lax.broadcasted_iota(jnp.int32, (32, 48), 1) - 8 - row
    bands = []
    for offset in (0, 1, -1):
        band = jnp.zeros((32, 48), jnp.float32)
        for d in range(-4, 5):
            if abs(2 * d + offset) <= REACH:
                band = band + jnp.where(shift == d, weight(2 * d + offset), 0.0)
        bands.append(band)
    return columns, bands


def step_kernel(flux_ref, noise_ref, prior_ref, table_ref, sound_ref, pick_ref, fp_ref, basis_ref,
                proposal_ref, predicted_ref, u_ref, v_ref,
                own_f, sib_f, tiles, halves, jac, jac_out, accs, extended, tab_v, tab_own, tab_sib,
                aug, parts, sums, full, work,
                load_sem, pair_send, pair_recv, tree_recv, cross_recv, tree_send, cross_send,
                jac_send, jac_recv, half_send, half_recv, halo_send, halo_recv,
                send_a, recv_a, send_b, recv_b, send_c, recv_c):
    t = lax.axis_index("tm")
    s = lax.axis_index("space")
    x, c = lax.div(t, 2), lax.rem(t, 2)
    y, z = lax.div(s, 8), lax.rem(s, 8)
    sibling = (x * 2 + (1 - c), s)
    z_up = (t, y * 8 + lax.rem(z + 1, 8))
    z_down = (t, y * 8 + lax.rem(z + 7, 8))
    y_up = (t, lax.rem(y + 1, 4) * 8 + z)
    y_down = (t, lax.rem(y + 3, 4) * 8 + z)
    x_up = (lax.rem(x + 1, 4) * 2 + c, s)
    x_down = (lax.rem(x + 3, 4) * 2 + c, s)
    count = BLOCKS_HERE

    own_load = pltpu.make_async_copy(
        basis_ref.at[:, pl.ds(pl.multiple_of(c * 128, 128), 128)], tiles.at[s], load_sem.at[0])
    own_load.start()
    fp_load = pltpu.make_async_copy(fp_ref.at[0], own_f.at[pl.ds(0, count)], load_sem.at[1])
    fp_load.start()
    tab_load = pltpu.make_async_copy(table_ref, tab_own, load_sem.at[2])
    tab_load.start()

    a = c * 8 + z
    b = x * 4 + y

    def in_a(k):
        other = lax.rem(a + k, 16)
        return other, (x * 2 + lax.div(other, 8), y * 8 + lax.rem(other, 8))

    def in_b(k):
        other = lax.rem(b + k, 16)
        return other, (lax.div(other, 4) * 2 + c, lax.rem(other, 4) * 8 + z)

    next_tile = (t, lax.rem(s + 1, 32))
    last_tile = (t, lax.rem(s + 31, 32))
    barrier = pltpu.get_barrier_semaphore()

    def greet(k, carry):
        for group in (in_a, in_b):
            pl.semaphore_signal(barrier, inc=1, device_id=group(k)[1], device_id_type=MESH)
        return carry

    lax.fori_loop(1, 16, greet, 0)
    for other in (next_tile, last_tile):
        pl.semaphore_signal(barrier, inc=1, device_id=other, device_id_type=MESH)
    pl.semaphore_wait(barrier, 32)

    to_next = pltpu.make_async_remote_copy(
        src_ref=noise_ref.at[pl.ds(24, 8)], dst_ref=extended.at[pl.ds(0, 8)], send_sem=halo_send.at[0],
        recv_sem=halo_recv.at[0], device_id=next_tile, device_id_type=MESH)
    to_last = pltpu.make_async_remote_copy(
        src_ref=noise_ref.at[pl.ds(0, 8)], dst_ref=extended.at[pl.ds(40, 8)], send_sem=halo_send.at[1],
        recv_sem=halo_recv.at[1], device_id=last_tile, device_id_type=MESH)

    @pl.when(s < 31)
    def _():
        to_next.start()

    @pl.when(s > 0)
    def _():
        to_last.start()

    tab_swap = pltpu.make_async_remote_copy(
        src_ref=table_ref, dst_ref=tab_v, send_sem=pair_send.at[0], recv_sem=pair_recv.at[0],
        device_id=sibling, device_id_type=MESH)
    tab_swap.start()
    own_load.wait()

    def send(rows, tile, send_sem, recv_sem, device):
        region = tiles.at[tile, rows]
        return pltpu.make_async_remote_copy(
            src_ref=region, dst_ref=region, send_sem=send_sem, recv_sem=recv_sem,
            device_id=device, device_id_type=MESH)

    classes = []
    start = 0
    for size, along_z_first, long_up in ((PA, True, True), (PB, True, False), (QA, False, True), (QB, False, False)):
        classes.append((pl.ds(start, size), along_z_first, long_up, False))
        start += size
    shared_base = start
    if RX:
        classes.append((pl.ds(pl.multiple_of(shared_base + x * RX, 16), RX), True, True, True))
    half = RX // 2

    def piece(owner, first, size):
        return pl.ds(pl.multiple_of(shared_base + owner * RX + first, 16), size)

    def tile_of(n):
        col, i = lax.div(n, 8), lax.rem(n, 8)
        dy = col + lax.div(col, 2) * (1 - 2 * lax.rem(col, 2))
        dz = lax.rem(lax.div(i + 1, 2) * (2 * lax.rem(i, 2) - 1) + 8, 8)
        tile = lax.rem(y - dy + 4, 4) * 8 + lax.rem(z - dz + 8, 8)
        return tile, dy, dz

    def forward(n):
        tile, dy, dz = tile_of(n)
        for k, (rows, along_z_first, long_up, shared) in enumerate(classes):
            hi_z, hi_y = (4, 2) if long_up else (3, 1)

            @pl.when(n > 0)
            def _():
                send(rows, tile, tree_send.at[k], tree_recv.at[k, tile], sibling).wait_recv()

            go_zu = jnp.logical_or(dz == 0, jnp.logical_and(dz >= 1, dz < hi_z))
            go_zd = jnp.logical_or(dz == 0, dz > hi_z + 1)
            go_yu = jnp.logical_or(dy == 0, jnp.logical_and(dy >= 1, dy < hi_y))
            go_yd = jnp.logical_or(dy == 0, dy > hi_y + 1)
            if along_z_first:
                go_zu, go_zd = jnp.logical_and(go_zu, dy == 0), jnp.logical_and(go_zd, dy == 0)
            else:
                go_yu, go_yd = jnp.logical_and(go_yu, dz == 0), jnp.logical_and(go_yd, dz == 0)
            for go, device in ((go_zu, z_up), (go_zd, z_down), (go_yu, y_up), (go_yd, y_down)):
                @pl.when(go)
                def _():
                    send(rows, tile, tree_send.at[k], tree_recv.at[k, tile], device).start()
            if shared:
                @pl.when(n > 0)
                def _():
                    send(rows, tile, cross_send.at[0], cross_recv.at[0, tile], x_up).start()
                    send(rows, tile, cross_send.at[1], cross_recv.at[1, tile], x_down).start()

    def send_half(tile, device):
        region = halves.at[tile]
        return pltpu.make_async_remote_copy(
            src_ref=region, dst_ref=region, send_sem=half_send, recv_sem=half_recv.at[tile],
            device_id=device, device_id_type=MESH)

    def forward_half(n):
        tile, dy, dz = tile_of(n)

        @pl.when(n > 0)
        def _():
            send_half(tile, sibling).wait_recv()

        for go, device in ((jnp.logical_and(dy == 0, dz < 4), z_up),
                           (jnp.logical_and(dy == 0, jnp.logical_or(dz == 0, dz > 5)), z_down),
                           (dy < 2, y_up), (dy == 0, y_down)):
            @pl.when(go)
            def _():
                send_half(tile, device).start()

    def pass_on(n):
        tile, _, _ = tile_of(n)
        below, above = lax.rem(x + 3, 4), lax.rem(x + 1, 4)
        send(piece(below, 0, RX), tile, cross_send.at[0], cross_recv.at[0, tile], sibling).wait_recv()
        send(piece(below, 0, half), tile, cross_send.at[2], cross_recv.at[2, tile], x_up).start()
        send(piece(above, 0, RX), tile, cross_send.at[1], cross_recv.at[1, tile], sibling).wait_recv()
        send(piece(above, half, half), tile, cross_send.at[3], cross_recv.at[3, tile], x_down).start()

    def multiply(n):
        tile, _, _ = tile_of(n)
        if RX:
            far = lax.rem(x + 2, 4)

            @pl.when(n > 0)
            def _():
                send(piece(far, 0, half), tile, cross_send.at[2], cross_recv.at[2, tile], sibling).wait_recv()
                send(piece(far, half, half), tile, cross_send.at[3], cross_recv.at[3, tile], sibling).wait_recv()
        own_a, own_b = tab_own[0, tile * 2], tab_own[0, tile * 2 + 1]
        sib_a, sib_b = tab_sib[0, tile * 2], tab_sib[0, tile * 2 + 1]
        total = jnp.zeros((128, 128), jnp.float32)
        for k in range(4096 // 512):
            ks = pl.ds(k * 512, 512)
            lhs = jnp.concatenate(
                [own_f[own_a, :, ks], own_f[own_b, :, ks], sib_f[sib_a, :, ks], sib_f[sib_b, :, ks]], axis=0)
            total += jnp.dot(lhs, tiles[tile, ks, :], preferred_element_type=jnp.float32)
        total = (total * JAC_SCALE).astype(jnp.bfloat16)
        values = halves[tile].astype(jnp.float32)
        seen_a = jnp.zeros((32, 128), jnp.float32)
        seen_b = jnp.zeros((32, 128), jnp.float32)
        for k in range(32):
            ks = pl.ds(k * 128, 128)
            value = values[k:k + 1, :]
            seen_a += own_f[own_a, :, ks].astype(jnp.float32) * value
            seen_b += own_f[own_b, :, ks].astype(jnp.float32) * value
        rows = pl.ds(pl.multiple_of(tile * 64, 64), 64)
        accs[rows, :] = jnp.concatenate([seen_a, seen_b], axis=0)
        jac[c, rows, :] = total[:64]
        jac_out[rows, :] = total[64:]
        pltpu.make_async_remote_copy(
            src_ref=jac_out.at[rows], dst_ref=jac.at[c, rows], send_sem=jac_send, recv_sem=jac_recv,
            device_id=sibling, device_id_type=MESH).start()

    forward(0)
    fp_swap = pltpu.make_async_remote_copy(
        src_ref=fp_ref.at[0], dst_ref=sib_f.at[pl.ds(0, count)], send_sem=pair_send.at[1],
        recv_sem=pair_recv.at[1], device_id=sibling, device_id_type=MESH)
    fp_swap.start()
    own_f[count] = jnp.zeros(own_f.shape[1:], own_f.dtype)
    sib_f[count] = jnp.zeros(sib_f.shape[1:], sib_f.dtype)
    columns, (band_even, band_up, band_down) = smoothing_matrices()
    extended[8:40, :] = noise_ref[...]

    @pl.when(s > 0)
    def _():
        to_next.wait_recv()

    @pl.when(s == 0)
    def _():
        extended[0:8, :] = jnp.zeros((8, 128), jnp.float32)

    @pl.when(s < 31)
    def _():
        to_last.wait_recv()

    @pl.when(s == 31)
    def _():
        extended[40:48, :] = jnp.zeros((8, 128), jnp.float32)

    def exact(p, q):
        return jnp.dot(p, q, precision=HIGHEST, preferred_element_type=jnp.float32)

    mixed = exact(extended[...], columns)
    swapped = jnp.concatenate([mixed[:, 64:], mixed[:, :64]], axis=1)
    lane = lax.broadcasted_iota(jnp.int32, (32, 128), 1)
    smooth = exact(band_even, mixed) + jnp.where(
        lane < 64, exact(band_up, swapped), exact(band_down, swapped))
    proposal = KEEP * flux_ref[...] + BETA * prior_ref[...] * smooth
    proposal_ref[...] = proposal
    halves[s] = proposal.astype(jnp.bfloat16)
    forward_half(0)
    tab_swap.wait()
    sib_load = pltpu.make_async_copy(tab_v, tab_sib, load_sem.at[3])
    sib_load.start()
    tab_load.wait()
    sib_load.wait()
    fp_load.wait()
    fp_swap.wait()

    def step(n, carry):
        @pl.when(n < 32)
        def _():
            forward(n)
            forward_half(n)
        if RX:
            @pl.when(jnp.logical_and(n >= LAG1 + 1, n < 32 + LAG1))
            def _():
                pass_on(n - LAG1)
        lag = LAG2 if RX else 0

        @pl.when(n >= lag)
        def _():
            multiply(n - lag)
        return carry

    if RX:
        lax.fori_loop(1, 32 + LAG2, step, 0)
    else:
        multiply(jnp.int32(0))
        lax.fori_loop(1, 32, step, 0)

    for k, (rows, _, _, _) in enumerate(classes):
        region = tiles.at[pl.ds(0, 31), rows]
        pltpu.make_async_copy(region, region, tree_send.at[k]).wait()
    if RX:
        for k, size in enumerate((RX, RX, half, half)):
            region = tiles.at[pl.ds(0, 31), pl.ds(0, size)]
            pltpu.make_async_copy(region, region, cross_send.at[k]).wait()
    whole = pltpu.make_async_remote_copy(
        src_ref=jac_out, dst_ref=jac.at[1 - c], send_sem=jac_send, recv_sem=jac_recv,
        device_id=sibling, device_id_type=MESH)
    whole.wait()
    region = halves.at[pl.ds(0, 31)]
    pltpu.make_async_copy(region, region, half_send).wait()

    @pl.when(s < 31)
    def _():
        to_next.wait_send()

    @pl.when(s > 0)
    def _():
        to_last.wait_send()

    low, high = jac[0], jac[1]

    def gram(a, b):
        return lax.dot_general(a, b, (((0,), (0,)), ((), ())), preferred_element_type=jnp.float32)

    aug[0:128, :] = gram(low, low)
    aug[128:256, :] = gram(low, high)
    aug[256:384, :] = gram(high, high)
    seen_rows = lax.dot_general(jnp.ones((8, 128), jnp.float32), accs[...], (((1,), (1,)), ((), ())),
                                precision=HIGHEST, preferred_element_type=jnp.float32)
    mis = sound_ref[...] - seen_rows
    mis_a = mis.astype(jnp.bfloat16)
    rest = mis - mis_a.astype(jnp.float32)
    mis_b = rest.astype(jnp.bfloat16)
    mis_c = (rest - mis_b.astype(jnp.float32)).astype(jnp.bfloat16)
    aug[384:, :] = jnp.zeros((128, 128), jnp.float32)
    for k, side in enumerate((low, high)):
        part = sum(jnp.dot(m, side, preferred_element_type=jnp.float32) for m in (mis_c, mis_b, mis_a))
        aug[384 + 8 * k:392 + 8 * k, :] = part

    def rows(index):
        return pl.ds(pl.multiple_of(index * 32, 32), 32)

    def scatter(k, carry):
        other, device = in_a(k)
        pltpu.make_async_remote_copy(
            src_ref=aug.at[rows(other)], dst_ref=parts.at[k - 1], send_sem=send_a, recv_sem=recv_a,
            device_id=device, device_id_type=MESH).start()
        return carry

    lax.fori_loop(1, 16, scatter, 0)

    def settle(region, send_sem, recv_sem):
        pltpu.make_async_copy(region, region, send_sem).wait()
        pltpu.make_async_copy(region, region, recv_sem).wait()

    seen = jnp.sum(accs[...].reshape(64, 32, 128), axis=-1)
    predicted_ref[...] = exact(pick_ref[...], seen)
    settle(parts, send_a, recv_a)
    own = aug[rows(a), :]
    for k in range(15):
        own = own + parts[k]
    sums[b] = own

    def exchange(k, carry):
        _, device = in_b(k)
        pltpu.make_async_remote_copy(
            src_ref=sums.at[b], dst_ref=sums.at[b], send_sem=send_b, recv_sem=recv_b,
            device_id=device, device_id_type=MESH).start()
        return carry

    lax.fori_loop(1, 16, exchange, 0)
    settle(parts, send_b, recv_b)
    total = sums[0]
    for k in range(1, 16):
        total = total + sums[k]
    full[rows(a), :] = total

    def spread(k, carry):
        _, device = in_a(k)
        pltpu.make_async_remote_copy(
            src_ref=full.at[rows(a)], dst_ref=full.at[rows(a)], send_sem=send_c, recv_sem=recv_c,
            device_id=device, device_id_type=MESH).start()
        return carry

    lax.fori_loop(1, 16, spread, 0)
    settle(parts, send_c, recv_c)
    square = (128, 128)
    eye = (lax.broadcasted_iota(jnp.int32, square, 0) == lax.broadcasted_iota(jnp.int32, square, 1))
    eye = eye.astype(jnp.float32)
    rhs = full[384:512, :].T
    work[0:128, 0:128] = full[0:128, :] + eye
    work[0:128, 128:256] = full[128:256, :]
    work[128:256, 128:256] = full[256:384, :] + eye
    work[0:128, 256:384] = rhs
    work[128:256, 256:384] = jnp.concatenate([rhs[:, 8:], rhs[:, :8]], axis=1)
    factor_rows(work, u_ref, v_ref)


def whole_step(flux, noise, prior, table, sound, pick, footprints, basis):
    vm = pl.BlockSpec(memory_space=pltpu.VMEM)
    hbm = pl.BlockSpec(memory_space=pl.ANY)
    dma = pltpu.SemaphoreType.DMA
    f32, bf16 = jnp.float32, jnp.bfloat16
    return pl.pallas_call(
        step_kernel,
        out_shape=(jax.ShapeDtypeStruct((32, 128), f32), jax.ShapeDtypeStruct((32, 32), f32),
                   jax.ShapeDtypeStruct((256, 256), f32), jax.ShapeDtypeStruct((256, 128), f32)),
        in_specs=[vm, vm, vm, vm, vm, vm, hbm, hbm],
        out_specs=(vm, vm, vm, vm),
        scratch_shapes=[
            pltpu.VMEM((33, 32, 4096), bf16), pltpu.VMEM((33, 32, 4096), bf16),
            pltpu.VMEM((32, 4096, 128), bf16), pltpu.VMEM((32, 32, 128), bf16),
            pltpu.VMEM((2, 2048, 128), bf16), pltpu.VMEM((2048, 128), bf16),
            pltpu.VMEM((2048, 128), f32), pltpu.VMEM((48, 128), f32),
            pltpu.VMEM((1, 128), jnp.int32), pltpu.SMEM((1, 128), jnp.int32), pltpu.SMEM((1, 128), jnp.int32),
            pltpu.VMEM((512, 128), f32), pltpu.VMEM((15, 32, 128), f32), pltpu.VMEM((16, 32, 128), f32),
            pltpu.VMEM((512, 128), f32), pltpu.VMEM((256, 384), f32),
            dma((4,)), dma((2,)), dma((2,)), dma((5, 32)), dma((4, 32)), dma((5,)), dma((4,)),
            dma, dma, dma, dma((32,)), dma((2,)), dma((2,)),
            dma, dma, dma, dma, dma, dma,
        ],
        compiler_params=pltpu.CompilerParams(
            collective_id=0, has_side_effects=True, vmem_limit_bytes=60 * 1024 * 1024),
        name="assimilate",
    )(flux, noise, prior, table, sound, pick, footprints, basis)


def per_device(flux, noise, prior_scale, footprints, soundings, targets, basis):
    block_count = footprints.shape[1]
    tile_count = 32
    destination = targets[0, :, 0]
    counts = (destination[:, None] == jnp.arange(tile_count)[None, :]).astype(jnp.int32)
    slot_rank = jnp.sum((jnp.cumsum(counts, axis=0) - counts) * counts, axis=1)
    slot_of = destination * 2 + slot_rank
    slot_match = slot_of[None, :] == jnp.arange(2 * tile_count)[:, None]
    source_of = jnp.sum(jnp.where(slot_match, jnp.arange(block_count)[None, :] + 1, 0), axis=1) - 1
    source_of = jnp.where(source_of < 0, block_count, source_of)
    table = jnp.zeros((1, 128), jnp.int32).at[0, : 2 * tile_count].set(source_of)
    pick = slot_match.T.astype(jnp.float32)
    sound = jnp.sum(jnp.where(slot_match[:, :, None], soundings[0].astype(jnp.float32)[None], 0.0), axis=1)
    proposal, predicted, factor_up, rhs_value = whole_step(
        flux.reshape(32, 128), noise.reshape(32, 128), prior_scale.reshape(32, 128),
        table, sound.reshape(1, 2048), pick, footprints, basis)
    return (proposal.reshape(1, 4096), predicted[None], factor_up, rhs_value[:, 0])


def solution(mesh):
    return jax.shard_map(
        per_device,
        mesh=mesh,
        in_specs=(
            P("tm", "space"),
            P("tm", "space"),
            P("space"),
            P("tm", "space", None, None),
            P("tm", "space", None),
            P("tm", "space", None),
            P("space", None),
        ),
        out_specs=(P("tm", "space"), P("tm", "space", None), P(), P()),
        check_vma=False,
    )
```

```python
import math

import jax
import jax.numpy as jnp
from jax import lax
from jax.experimental import pallas as pl
from jax.experimental.pallas import tpu as pltpu
from jax.sharding import PartitionSpec as P

MESH = pl.DeviceIdType.MESH
HIGHEST = lax.Precision.HIGHEST
BLOCKS_HERE = 32
JAC_SCALE = float(262144) ** (-0.5)
REACH = 8
BETA = 0.6
KEEP = 0.8


def kernel_weights(reach):
    profile = [(1.0 + 2.0 * abs(d) / reach) * math.exp(-2.0 * abs(d) / reach) for d in range(-reach, reach + 1)]
    norm = math.sqrt(sum(p * p for p in profile))
    return [p / norm for p in profile]


KERNEL = kernel_weights(REACH)


def factor_rows(work, out_u, out_v):
    row = lax.broadcasted_iota(jnp.int32, (32, 128), 0)
    lane = lax.broadcasted_iota(jnp.int32, (32, 128), 1)
    wide_row = lax.broadcasted_iota(jnp.int32, (32, 256), 0)
    wide_lane = lax.broadcasted_iota(jnp.int32, (32, 256), 1)
    for k in range(8):
        k0, c0 = 32 * k, 128 * (k // 4)
        off = k0 - c0
        eye0 = (off + 64) % 128
        rows = work[k0:k0 + 32, :]
        e = jnp.where(jnp.logical_and(lane >= off, lane < off + 32), rows[:, c0:c0 + 128], 0.0)
        e = e + (lane - eye0 == row).astype(jnp.float32)
        for j in range(0, 32, 8):
            cols = [jnp.broadcast_to(e[:, off + p:off + p + 1], (32, 128)) for p in range(j, j + 8)]
            heads = [e[p:p + 1, :] for p in range(j, j + 8)]
            for i in range(8):
                p = j + i
                scale = 1.0 / cols[i][p:p + 1, :]
                below = jnp.where(row > p, cols[i], 0.0)
                scaled = heads[i] * scale
                for l in range(i + 1, 8):
                    heads[l] = heads[l] - cols[i][j + l:j + l + 1, :] * scaled
                    cols[l] = cols[l] - below * (cols[l][p:p + 1, :] * scale)
                e = e - below * scaled
        diagonal = jnp.sum(jnp.where(lane == row + off, e, 0.0), axis=1, keepdims=True)
        e = e * lax.rsqrt(diagonal)
        inverse = e[:, eye0:eye0 + 32]
        panel = jnp.dot(inverse, rows[:, c0:], preferred_element_type=jnp.float32, precision=HIGHEST)
        upper = panel[:, :256 - c0]
        if c0:
            upper = jnp.concatenate([jnp.zeros((32, c0), jnp.float32), upper], axis=1)
        upper = jnp.where(wide_lane >= wide_row + k0, upper, 0.0)
        out_u[k0:k0 + 32, :] = upper
        out_v[k0:k0 + 32, :] = panel[:, 256 - c0:]
        if k < 7:
            k1 = k0 + 32
            c1 = 128 * (k1 // 128)
            left = panel[:, c1 - c0:256 - c0]
            update = lax.dot_general(left, panel[:, c1 - c0:], (((0,), (0,)), ((), ())),
                                     preferred_element_type=jnp.float32, precision=HIGHEST)
            work[k1:, c1:] = work[k1:, c1:] - update[k1 - c1:]


PA, PB, QA, QB = 368, 816, 560, 560
RX = 448
LAG1, LAG2 = 2, 4


def weight(position):
    return KERNEL[REACH + position]


def slot_tables(target):
    row = lax.broadcasted_iota(jnp.int32, (32, 32), 0)
    lane = lax.broadcasted_iota(jnp.int32, (32, 32), 1)
    across = jnp.broadcast_to(target, (32, 32))
    down = jnp.sum(jnp.where(row == lane, across, 0), axis=1, keepdims=True)
    earlier = jnp.logical_and(across == down, lane < row)
    slot = 2 * down + jnp.sum(jnp.where(earlier, 1, 0), axis=1, keepdims=True)
    slots = lax.broadcasted_iota(jnp.int32, (32, 128), 1)
    block = lax.broadcasted_iota(jnp.int32, (32, 128), 0)
    match = slot == slots
    source = 32 + jnp.sum(jnp.where(match, block - 32, 0), axis=0, keepdims=True)
    return source, jnp.where(match, 1.0, 0.0)


def smoothing_matrices():
    lane = lax.broadcasted_iota(jnp.int32, (128, 128), 1)
    source = lax.broadcasted_iota(jnp.int32, (128, 128), 0)
    same = lax.div(lane, 64) == lax.div(source, 64)
    gap = lax.rem(source - lane + 64 + REACH, 64)
    columns = jnp.zeros((128, 128), jnp.float32)
    for b in range(-REACH, REACH + 1):
        columns = columns + jnp.where(jnp.logical_and(same, gap == b + REACH), weight(b), 0.0)
    row = lax.broadcasted_iota(jnp.int32, (32, 48), 0)
    shift = lax.broadcasted_iota(jnp.int32, (32, 48), 1) - 8 - row
    bands = []
    for offset in (0, 1, -1):
        band = jnp.zeros((32, 48), jnp.float32)
        for d in range(-4, 5):
            if abs(2 * d + offset) <= REACH:
                band = band + jnp.where(shift == d, weight(2 * d + offset), 0.0)
        bands.append(band)
    return columns, bands


def step_kernel(flux_ref, noise_ref, prior_ref, target_ref, sound_ref, fp_ref, basis_ref,
                proposal_ref, predicted_ref, full,
                own_f, sib_f, tiles, halves, jac, jac_out, accs, gaps, extended, square, sound_t,
                tab_mine, tab_v, tab_own, tab_sib, aug, parts, sums,
                load_sem, pair_send, pair_recv, tree_recv, cross_recv, tree_send, cross_send,
                jac_send, jac_recv, half_send, half_recv, halo_send, halo_recv,
                send_a, recv_a, send_b, recv_b, send_c, recv_c):
    t = lax.axis_index("tm")
    s = lax.axis_index("space")
    x, c = lax.div(t, 2), lax.rem(t, 2)
    y, z = lax.div(s, 8), lax.rem(s, 8)
    sibling = (x * 2 + (1 - c), s)
    z_up = (t, y * 8 + lax.rem(z + 1, 8))
    z_down = (t, y * 8 + lax.rem(z + 7, 8))
    y_up = (t, lax.rem(y + 1, 4) * 8 + z)
    y_down = (t, lax.rem(y + 3, 4) * 8 + z)
    x_up = (lax.rem(x + 1, 4) * 2 + c, s)
    x_down = (lax.rem(x + 3, 4) * 2 + c, s)
    count = BLOCKS_HERE

    own_load = pltpu.make_async_copy(
        basis_ref.at[:, pl.ds(pl.multiple_of(c * 128, 128), 128)], tiles.at[s], load_sem.at[0])
    own_load.start()
    fp_load = pltpu.make_async_copy(fp_ref.at[0], own_f.at[pl.ds(0, count)], load_sem.at[1])
    fp_load.start()

    a = t * 4 + y
    b = z

    def in_a(k):
        other = lax.rem(a + k, 32)
        return other, (lax.div(other, 4), lax.rem(other, 4) * 8 + z)

    def in_b(k):
        other = lax.rem(b + k, 8)
        return other, (t, y * 8 + other)

    next_tile = (t, lax.rem(s + 1, 32))
    last_tile = (t, lax.rem(s + 31, 32))
    barrier = pltpu.get_barrier_semaphore()

    def greet_a(k, carry):
        pl.semaphore_signal(barrier, inc=1, device_id=in_a(k)[1], device_id_type=MESH)
        return carry

    def greet_b(k, carry):
        pl.semaphore_signal(barrier, inc=1, device_id=in_b(k)[1], device_id_type=MESH)
        return carry

    lax.fori_loop(1, 32, greet_a, 0)
    lax.fori_loop(1, 8, greet_b, 0)
    for other in (next_tile, last_tile):
        pl.semaphore_signal(barrier, inc=1, device_id=other, device_id_type=MESH)
    pl.semaphore_wait(barrier, 40)

    to_next = pltpu.make_async_remote_copy(
        src_ref=noise_ref.at[pl.ds(24, 8)], dst_ref=extended.at[pl.ds(0, 8)], send_sem=halo_send.at[0],
        recv_sem=halo_recv.at[0], device_id=next_tile, device_id_type=MESH)
    to_last = pltpu.make_async_remote_copy(
        src_ref=noise_ref.at[pl.ds(0, 8)], dst_ref=extended.at[pl.ds(40, 8)], send_sem=halo_send.at[1],
        recv_sem=halo_recv.at[1], device_id=last_tile, device_id_type=MESH)

    @pl.when(s < 31)
    def _():
        to_next.start()

    @pl.when(s > 0)
    def _():
        to_last.start()

    own_load.wait()

    def send(rows, tile, send_sem, recv_sem, device):
        region = tiles.at[tile, rows]
        return pltpu.make_async_remote_copy(
            src_ref=region, dst_ref=region, send_sem=send_sem, recv_sem=recv_sem,
            device_id=device, device_id_type=MESH)

    classes = []
    start = 0
    for size, along_z_first, long_up in ((PA, True, True), (PB, True, False), (QA, False, True), (QB, False, False)):
        classes.append((pl.ds(start, size), along_z_first, long_up, False))
        start += size
    shared_base = start
    if RX:
        classes.append((pl.ds(pl.multiple_of(shared_base + x * RX, 16), RX), True, True, True))
    half = RX // 2

    def piece(owner, first, size):
        return pl.ds(pl.multiple_of(shared_base + owner * RX + first, 16), size)

    def tile_of(n):
        col, i = lax.div(n, 8), lax.rem(n, 8)
        dy = col + lax.div(col, 2) * (1 - 2 * lax.rem(col, 2))
        dz = lax.rem(lax.div(i + 1, 2) * (2 * lax.rem(i, 2) - 1) + 8, 8)
        tile = lax.rem(y - dy + 4, 4) * 8 + lax.rem(z - dz + 8, 8)
        return tile, dy, dz

    def forward(n):
        tile, dy, dz = tile_of(n)
        for k, (rows, along_z_first, long_up, shared) in enumerate(classes):
            hi_z, hi_y = (4, 2) if long_up else (3, 1)

            @pl.when(n > 0)
            def _():
                send(rows, tile, tree_send.at[k], tree_recv.at[k, tile], sibling).wait_recv()

            go_zu = jnp.logical_or(dz == 0, jnp.logical_and(dz >= 1, dz < hi_z))
            go_zd = jnp.logical_or(dz == 0, dz > hi_z + 1)
            go_yu = jnp.logical_or(dy == 0, jnp.logical_and(dy >= 1, dy < hi_y))
            go_yd = jnp.logical_or(dy == 0, dy > hi_y + 1)
            if along_z_first:
                go_zu, go_zd = jnp.logical_and(go_zu, dy == 0), jnp.logical_and(go_zd, dy == 0)
            else:
                go_yu, go_yd = jnp.logical_and(go_yu, dz == 0), jnp.logical_and(go_yd, dz == 0)
            for go, device in ((go_zu, z_up), (go_zd, z_down), (go_yu, y_up), (go_yd, y_down)):
                @pl.when(go)
                def _():
                    send(rows, tile, tree_send.at[k], tree_recv.at[k, tile], device).start()
            if shared:
                @pl.when(n > 0)
                def _():
                    send(rows, tile, cross_send.at[0], cross_recv.at[0, tile], x_up).start()
                    send(rows, tile, cross_send.at[1], cross_recv.at[1, tile], x_down).start()

    def send_half(tile, device):
        region = halves.at[tile]
        return pltpu.make_async_remote_copy(
            src_ref=region, dst_ref=region, send_sem=half_send, recv_sem=half_recv.at[tile],
            device_id=device, device_id_type=MESH)

    def forward_half(n):
        tile, dy, dz = tile_of(n)

        @pl.when(n > 0)
        def _():
            send_half(tile, sibling).wait_recv()

        for go, device in ((jnp.logical_and(dy == 0, dz < 4), z_up),
                           (jnp.logical_and(dy == 0, jnp.logical_or(dz == 0, dz > 5)), z_down),
                           (dy < 2, y_up), (dy == 0, y_down)):
            @pl.when(go)
            def _():
                send_half(tile, device).start()

    def pass_on(n):
        tile, _, _ = tile_of(n)
        below, above = lax.rem(x + 3, 4), lax.rem(x + 1, 4)
        send(piece(below, 0, RX), tile, cross_send.at[0], cross_recv.at[0, tile], sibling).wait_recv()
        send(piece(below, 0, half), tile, cross_send.at[2], cross_recv.at[2, tile], x_up).start()
        send(piece(above, 0, RX), tile, cross_send.at[1], cross_recv.at[1, tile], sibling).wait_recv()
        send(piece(above, half, half), tile, cross_send.at[3], cross_recv.at[3, tile], x_down).start()

    def multiply(n):
        tile, _, _ = tile_of(n)
        if RX:
            far = lax.rem(x + 2, 4)

            @pl.when(n > 0)
            def _():
                send(piece(far, 0, half), tile, cross_send.at[2], cross_recv.at[2, tile], sibling).wait_recv()
                send(piece(far, half, half), tile, cross_send.at[3], cross_recv.at[3, tile], sibling).wait_recv()
        own_a, own_b = tab_own[0, tile * 2], tab_own[0, tile * 2 + 1]
        sib_a, sib_b = tab_sib[0, tile * 2], tab_sib[0, tile * 2 + 1]
        total = jnp.zeros((128, 128), jnp.float32)
        for k in range(4096 // 512):
            ks = pl.ds(k * 512, 512)
            lhs = jnp.concatenate(
                [own_f[own_a, :, ks], own_f[own_b, :, ks], sib_f[sib_a, :, ks], sib_f[sib_b, :, ks]], axis=0)
            total += jnp.dot(lhs, tiles[tile, ks, :], preferred_element_type=jnp.float32)
        total = (total * JAC_SCALE).astype(jnp.bfloat16)
        values = halves[tile].astype(jnp.float32)
        seen_a = jnp.zeros((32, 128), jnp.float32)
        seen_b = jnp.zeros((32, 128), jnp.float32)
        for k in range(32):
            ks = pl.ds(k * 128, 128)
            value = values[k:k + 1, :]
            seen_a += own_f[own_a, :, ks].astype(jnp.float32) * value
            seen_b += own_f[own_b, :, ks].astype(jnp.float32) * value
        rows = pl.ds(pl.multiple_of(tile * 64, 64), 64)
        accs[rows, :] = jnp.concatenate([seen_a, seen_b], axis=0)
        lane = lax.broadcasted_iota(jnp.int32, (32, 128), 1)
        gaps[rows, :] = jnp.concatenate(
            [jnp.where(lane == own_a, sound_t[...], 0.0) - seen_a,
             jnp.where(lane == own_b, sound_t[...], 0.0) - seen_b], axis=0)
        jac[c, rows, :] = total[:64]
        jac_out[rows, :] = total[64:]
        pltpu.make_async_remote_copy(
            src_ref=jac_out.at[rows], dst_ref=jac.at[c, rows], send_sem=jac_send, recv_sem=jac_recv,
            device_id=sibling, device_id_type=MESH).start()

    forward(0)
    source, match = slot_tables(target_ref[...])
    tab_mine[...] = source
    tab_load = pltpu.make_async_copy(tab_mine, tab_own, load_sem.at[2])
    tab_load.start()
    tab_swap = pltpu.make_async_remote_copy(
        src_ref=tab_mine, dst_ref=tab_v, send_sem=pair_send.at[0], recv_sem=pair_recv.at[0],
        device_id=sibling, device_id_type=MESH)
    tab_swap.start()
    square[...] = jnp.zeros(square.shape, jnp.float32)
    square[0:32, 0:32] = sound_ref[...].astype(jnp.float32)
    sound_t[...] = square[...].T[0:32, :]
    fp_swap = pltpu.make_async_remote_copy(
        src_ref=fp_ref.at[0], dst_ref=sib_f.at[pl.ds(0, count)], send_sem=pair_send.at[1],
        recv_sem=pair_recv.at[1], device_id=sibling, device_id_type=MESH)
    fp_swap.start()
    own_f[count] = jnp.zeros(own_f.shape[1:], own_f.dtype)
    sib_f[count] = jnp.zeros(sib_f.shape[1:], sib_f.dtype)
    columns, (band_even, band_up, band_down) = smoothing_matrices()
    extended[8:40, :] = noise_ref[...]

    @pl.when(s > 0)
    def _():
        to_next.wait_recv()

    @pl.when(s == 0)
    def _():
        extended[0:8, :] = jnp.zeros((8, 128), jnp.float32)

    @pl.when(s < 31)
    def _():
        to_last.wait_recv()

    @pl.when(s == 31)
    def _():
        extended[40:48, :] = jnp.zeros((8, 128), jnp.float32)

    def exact(p, q):
        return jnp.dot(p, q, precision=HIGHEST, preferred_element_type=jnp.float32)

    mixed = exact(extended[...], columns)
    swapped = jnp.concatenate([mixed[:, 64:], mixed[:, :64]], axis=1)
    lane = lax.broadcasted_iota(jnp.int32, (32, 128), 1)
    smooth = exact(band_even, mixed) + jnp.where(
        lane < 64, exact(band_up, swapped), exact(band_down, swapped))
    proposal = KEEP * flux_ref[...] + BETA * prior_ref[...] * smooth
    proposal_ref[...] = proposal
    halves[s] = proposal.astype(jnp.bfloat16)
    forward_half(0)
    tab_swap.wait()
    sib_load = pltpu.make_async_copy(tab_v, tab_sib, load_sem.at[3])
    sib_load.start()
    tab_load.wait()
    sib_load.wait()
    fp_load.wait()
    fp_swap.wait()

    def step(n, carry):
        @pl.when(n < 32)
        def _():
            forward(n)
            forward_half(n)
        if RX:
            @pl.when(jnp.logical_and(n >= LAG1 + 1, n < 32 + LAG1))
            def _():
                pass_on(n - LAG1)
        lag = LAG2 if RX else 0

        @pl.when(n >= lag)
        def _():
            multiply(n - lag)
        return carry

    if RX:
        lax.fori_loop(1, 32 + LAG2, step, 0)
    else:
        multiply(jnp.int32(0))
        lax.fori_loop(1, 32, step, 0)

    for k, (rows, _, _, _) in enumerate(classes):
        region = tiles.at[pl.ds(0, 31), rows]
        pltpu.make_async_copy(region, region, tree_send.at[k]).wait()
    if RX:
        for k, size in enumerate((RX, RX, half, half)):
            region = tiles.at[pl.ds(0, 31), pl.ds(0, size)]
            pltpu.make_async_copy(region, region, cross_send.at[k]).wait()
    whole = pltpu.make_async_remote_copy(
        src_ref=jac_out, dst_ref=jac.at[1 - c], send_sem=jac_send, recv_sem=jac_recv,
        device_id=sibling, device_id_type=MESH)
    whole.wait()
    region = halves.at[pl.ds(0, 31)]
    pltpu.make_async_copy(region, region, half_send).wait()

    @pl.when(s < 31)
    def _():
        to_next.wait_send()

    @pl.when(s > 0)
    def _():
        to_last.wait_send()

    low, high = jac[0], jac[1]

    def gram(a, b):
        return lax.dot_general(a, b, (((0,), (0,)), ((), ())), preferred_element_type=jnp.float32)

    aug[0:128, :] = gram(low, low)
    aug[128:256, :] = gram(low, high)
    aug[256:384, :] = gram(high, high)
    mis = lax.dot_general(jnp.ones((8, 128), jnp.float32), gaps[...], (((1,), (1,)), ((), ())),
                          precision=HIGHEST, preferred_element_type=jnp.float32)
    mis_a = mis.astype(jnp.bfloat16)
    rest = mis - mis_a.astype(jnp.float32)
    mis_b = rest.astype(jnp.bfloat16)
    mis_c = (rest - mis_b.astype(jnp.float32)).astype(jnp.bfloat16)
    aug[384:, :] = jnp.zeros((128, 128), jnp.float32)
    for k, side in enumerate((low, high)):
        part = sum(jnp.dot(m, side, preferred_element_type=jnp.float32) for m in (mis_c, mis_b, mis_a))
        aug[384 + 8 * k:392 + 8 * k, :] = part

    def rows(index):
        return pl.ds(pl.multiple_of(index * 16, 16), 16)

    def scatter(k, carry):
        other, device = in_a(k)
        pltpu.make_async_remote_copy(
            src_ref=aug.at[rows(other)], dst_ref=parts.at[k - 1], send_sem=send_a, recv_sem=recv_a,
            device_id=device, device_id_type=MESH).start()
        return carry

    lax.fori_loop(1, 32, scatter, 0)

    def settle(region, send_sem, recv_sem):
        pltpu.make_async_copy(region, region, send_sem).wait()
        pltpu.make_async_copy(region, region, recv_sem).wait()

    seen = jnp.sum(accs[...].reshape(64, 32, 128), axis=-1)
    predicted_ref[...] = exact(match[:, :64], seen)
    settle(parts, send_a, recv_a)
    own = aug[rows(a), :]
    for k in range(31):
        own = own + parts[k]
    sums[b] = own

    def exchange(k, carry):
        _, device = in_b(k)
        pltpu.make_async_remote_copy(
            src_ref=sums.at[b], dst_ref=sums.at[b], send_sem=send_b, recv_sem=recv_b,
            device_id=device, device_id_type=MESH).start()
        return carry

    lax.fori_loop(1, 8, exchange, 0)
    settle(parts.at[pl.ds(0, 7)], send_b, recv_b)
    total = sums[0]
    for k in range(1, 8):
        total = total + sums[k]
    full[rows(a), :] = total

    def spread(k, carry):
        _, device = in_a(k)
        pltpu.make_async_remote_copy(
            src_ref=full.at[rows(a)], dst_ref=full.at[rows(a)], send_sem=send_c, recv_sem=recv_c,
            device_id=device, device_id_type=MESH).start()
        return carry

    lax.fori_loop(1, 32, spread, 0)
    settle(parts, send_c, recv_c)


def factor_kernel(full, proposal_in, predicted_in, proposal_ref, predicted_ref, u_ref, v_ref, work, solved):
    proposal_ref[...] = proposal_in[...]
    predicted_ref[...] = predicted_in[...]
    square = (128, 128)
    eye = (lax.broadcasted_iota(jnp.int32, square, 0) == lax.broadcasted_iota(jnp.int32, square, 1))
    eye = eye.astype(jnp.float32)
    rhs = full[384:512, :].T
    work[0:128, 0:128] = full[0:128, :] + eye
    work[0:128, 128:256] = full[128:256, :]
    work[128:256, 128:256] = full[256:384, :] + eye
    work[0:128, 256:384] = rhs
    work[128:256, 256:384] = jnp.concatenate([rhs[:, 8:], rhs[:, :8]], axis=1)
    factor_rows(work, u_ref, solved)
    v_ref[:, 0:128] = solved[0:128, :].T[0:1, :]
    v_ref[:, 128:256] = solved[128:256, :].T[0:1, :]


def whole_step(flux, noise, prior, target, sound, footprints, basis):
    vm = pl.BlockSpec(memory_space=pltpu.VMEM)
    hbm = pl.BlockSpec(memory_space=pl.ANY)
    dma = pltpu.SemaphoreType.DMA
    f32, bf16, i32 = jnp.float32, jnp.bfloat16, jnp.int32
    shapes = (jax.ShapeDtypeStruct((32, 128), f32), jax.ShapeDtypeStruct((32, 32), f32))
    proposal, predicted, summed = pl.pallas_call(
        step_kernel,
        out_shape=shapes + (jax.ShapeDtypeStruct((512, 128), f32),),
        in_specs=[vm, vm, vm, vm, vm, hbm, hbm],
        out_specs=(vm, vm, vm),
        scratch_shapes=[
            pltpu.VMEM((33, 32, 4096), bf16), pltpu.VMEM((33, 32, 4096), bf16),
            pltpu.VMEM((32, 4096, 128), bf16), pltpu.VMEM((32, 32, 128), bf16),
            pltpu.VMEM((2, 2048, 128), bf16), pltpu.VMEM((2048, 128), bf16),
            pltpu.VMEM((2048, 128), f32), pltpu.VMEM((2048, 128), f32), pltpu.VMEM((48, 128), f32),
            pltpu.VMEM((128, 128), f32), pltpu.VMEM((32, 128), f32),
            pltpu.VMEM((1, 128), i32), pltpu.VMEM((1, 128), i32), pltpu.SMEM((1, 128), i32), pltpu.SMEM((1, 128), i32),
            pltpu.VMEM((512, 128), f32), pltpu.VMEM((31, 16, 128), f32), pltpu.VMEM((8, 16, 128), f32),
            dma((4,)), dma((2,)), dma((2,)), dma((5, 32)), dma((4, 32)), dma((5,)), dma((4,)),
            dma, dma, dma, dma((32,)), dma((2,)), dma((2,)),
            dma, dma, dma, dma, dma, dma,
        ],
        compiler_params=pltpu.CompilerParams(
            collective_id=0, has_side_effects=True, vmem_limit_bytes=60 * 1024 * 1024),
        name="assimilate",
    )(flux, noise, prior, target, sound, footprints, basis)
    return pl.pallas_call(
        factor_kernel,
        out_shape=shapes + (jax.ShapeDtypeStruct((256, 256), f32), jax.ShapeDtypeStruct((1, 256), f32)),
        in_specs=[vm, vm, vm],
        out_specs=(vm, vm, vm, vm),
        scratch_shapes=[pltpu.VMEM((256, 384), f32), pltpu.VMEM((256, 128), f32)],
        name="factor",
    )(summed, proposal, predicted)


def per_device(flux, noise, prior_scale, footprints, soundings, targets, basis):
    proposal, predicted, factor_up, rhs_value = whole_step(
        flux.reshape(32, 128), noise.reshape(32, 128), prior_scale.reshape(32, 128),
        targets.reshape(1, 32), soundings.reshape(32, 32), footprints, basis)
    return (proposal.reshape(1, 4096), predicted[None], factor_up, rhs_value.reshape(256))


def solution(mesh):
    return jax.shard_map(
        per_device,
        mesh=mesh,
        in_specs=(
            P("tm", "space"),
            P("tm", "space"),
            P("space"),
            P("tm", "space", None, None),
            P("tm", "space", None),
            P("tm", "space", None),
            P("space", None),
        ),
        out_specs=(P("tm", "space"), P("tm", "space", None), P(), P()),
        check_vma=False,
    )
```

```python
import math

import jax
import jax.numpy as jnp
from jax import lax
from jax.experimental import pallas as pl
from jax.experimental.pallas import tpu as pltpu
from jax.sharding import PartitionSpec as P

MESH = pl.DeviceIdType.MESH
HIGHEST = lax.Precision.HIGHEST
BLOCKS_HERE = 32
JAC_SCALE = float(262144) ** (-0.5)
REACH = 8
BETA = 0.6
KEEP = 0.8


def kernel_weights(reach):
    profile = [(1.0 + 2.0 * abs(d) / reach) * math.exp(-2.0 * abs(d) / reach) for d in range(-reach, reach + 1)]
    norm = math.sqrt(sum(p * p for p in profile))
    return [p / norm for p in profile]


KERNEL = kernel_weights(REACH)


def factor_rows(work, out_u, out_v):
    row = lax.broadcasted_iota(jnp.int32, (32, 128), 0)
    lane = lax.broadcasted_iota(jnp.int32, (32, 128), 1)
    wide_row = lax.broadcasted_iota(jnp.int32, (32, 256), 0)
    wide_lane = lax.broadcasted_iota(jnp.int32, (32, 256), 1)
    for k in range(8):
        k0, c0 = 32 * k, 128 * (k // 4)
        off = k0 - c0
        eye0 = (off + 64) % 128
        rows = work[k0:k0 + 32, :]
        e = jnp.where(jnp.logical_and(lane >= off, lane < off + 32), rows[:, c0:c0 + 128], 0.0)
        e = e + (lane - eye0 == row).astype(jnp.float32)
        for j in range(0, 32, 8):
            cols = [jnp.broadcast_to(e[:, off + p:off + p + 1], (32, 128)) for p in range(j, j + 8)]
            heads = [e[p:p + 1, :] for p in range(j, j + 8)]
            for i in range(8):
                p = j + i
                scale = 1.0 / cols[i][p:p + 1, :]
                below = jnp.where(row > p, cols[i], 0.0)
                scaled = heads[i] * scale
                for l in range(i + 1, 8):
                    heads[l] = heads[l] - cols[i][j + l:j + l + 1, :] * scaled
                    cols[l] = cols[l] - below * (cols[l][p:p + 1, :] * scale)
                e = e - below * scaled
        diagonal = jnp.sum(jnp.where(lane == row + off, e, 0.0), axis=1, keepdims=True)
        e = e * lax.rsqrt(diagonal)
        inverse = e[:, eye0:eye0 + 32]
        panel = jnp.dot(inverse, rows[:, c0:], preferred_element_type=jnp.float32, precision=HIGHEST)
        upper = panel[:, :256 - c0]
        if c0:
            upper = jnp.concatenate([jnp.zeros((32, c0), jnp.float32), upper], axis=1)
        upper = jnp.where(wide_lane >= wide_row + k0, upper, 0.0)
        out_u[k0:k0 + 32, :] = upper
        out_v[k0:k0 + 32, :] = panel[:, 256 - c0:]
        if k < 7:
            k1 = k0 + 32
            c1 = 128 * (k1 // 128)
            left = panel[:, c1 - c0:256 - c0]
            update = lax.dot_general(left, panel[:, c1 - c0:], (((0,), (0,)), ((), ())),
                                     preferred_element_type=jnp.float32, precision=HIGHEST)
            work[k1:, c1:] = work[k1:, c1:] - update[k1 - c1:]


PA, PB, QA, QB = 512, 896, 576, 576
RX = 384
AHEAD_SHARED, AHEAD_ACROSS = 6, 0
LAG_CROSS, LAG_WORK = 3, 2


def weight(position):
    return KERNEL[REACH + position]


def slot_tables(target):
    row = lax.broadcasted_iota(jnp.int32, (32, 32), 0)
    lane = lax.broadcasted_iota(jnp.int32, (32, 32), 1)
    across = jnp.broadcast_to(target, (32, 32))
    down = jnp.sum(jnp.where(row == lane, across, 0), axis=1, keepdims=True)
    earlier = jnp.logical_and(across == down, lane < row)
    slot = 2 * down + jnp.sum(jnp.where(earlier, 1, 0), axis=1, keepdims=True)
    slots = lax.broadcasted_iota(jnp.int32, (32, 128), 1)
    block = lax.broadcasted_iota(jnp.int32, (32, 128), 0)
    match = slot == slots
    source = 32 + jnp.sum(jnp.where(match, block - 32, 0), axis=0, keepdims=True)
    return source, jnp.where(match, 1.0, 0.0)


def smoothing_matrices():
    lane = lax.broadcasted_iota(jnp.int32, (128, 128), 1)
    source = lax.broadcasted_iota(jnp.int32, (128, 128), 0)
    same = lax.div(lane, 64) == lax.div(source, 64)
    gap = lax.rem(source - lane + 64 + REACH, 64)
    columns = jnp.zeros((128, 128), jnp.float32)
    for b in range(-REACH, REACH + 1):
        columns = columns + jnp.where(jnp.logical_and(same, gap == b + REACH), weight(b), 0.0)
    row = lax.broadcasted_iota(jnp.int32, (32, 48), 0)
    shift = lax.broadcasted_iota(jnp.int32, (32, 48), 1) - 8 - row
    bands = []
    for offset in (0, 1, -1):
        band = jnp.zeros((32, 48), jnp.float32)
        for d in range(-4, 5):
            if abs(2 * d + offset) <= REACH:
                band = band + jnp.where(shift == d, weight(2 * d + offset), 0.0)
        bands.append(band)
    return columns, bands


def step_kernel(flux_ref, noise_ref, prior_ref, target_ref, sound_ref, fp_ref, basis_ref,
                proposal_ref, predicted_ref, full,
                own_f, sib_f, tiles, halves, jac, jac_out, accs, gaps, extended, square, sound_t,
                tab_mine, tab_v, tab_own, tab_sib, aug, parts, sums, accum,
                load_sem, pair_send, pair_recv, tree_recv, cross_recv, tree_send, cross_send,
                jac_send, jac_recv, half_send, half_recv, halo_send, halo_recv,
                send_a, recv_a, send_b, recv_b, send_c, recv_c):
    t = lax.axis_index("tm")
    s = lax.axis_index("space")
    x, c = lax.div(t, 2), lax.rem(t, 2)
    y, z = lax.div(s, 8), lax.rem(s, 8)
    sibling = (x * 2 + (1 - c), s)
    z_up = (t, y * 8 + lax.rem(z + 1, 8))
    z_down = (t, y * 8 + lax.rem(z + 7, 8))
    y_up = (t, lax.rem(y + 1, 4) * 8 + z)
    y_down = (t, lax.rem(y + 3, 4) * 8 + z)
    x_up = (lax.rem(x + 1, 4) * 2 + c, s)
    x_down = (lax.rem(x + 3, 4) * 2 + c, s)
    count = BLOCKS_HERE

    own_load = pltpu.make_async_copy(
        basis_ref.at[:, pl.ds(pl.multiple_of(c * 128, 128), 128)], tiles.at[s], load_sem.at[0])
    own_load.start()
    fp_load = pltpu.make_async_copy(fp_ref.at[0], own_f.at[pl.ds(0, count)], load_sem.at[1])
    fp_load.start()

    a = t * 4 + y
    b = z

    def in_a(k):
        other = lax.rem(a + k, 32)
        return other, (lax.div(other, 4), lax.rem(other, 4) * 8 + z)

    def in_b(k):
        other = lax.rem(b + k, 8)
        return other, (t, y * 8 + other)

    next_tile = (t, lax.rem(s + 1, 32))
    last_tile = (t, lax.rem(s + 31, 32))
    barrier = pltpu.get_barrier_semaphore()

    def greet_a(k, carry):
        pl.semaphore_signal(barrier, inc=1, device_id=in_a(k)[1], device_id_type=MESH)
        return carry

    def greet_b(k, carry):
        pl.semaphore_signal(barrier, inc=1, device_id=in_b(k)[1], device_id_type=MESH)
        return carry

    lax.fori_loop(1, 32, greet_a, 0)
    lax.fori_loop(1, 8, greet_b, 0)
    for other in (next_tile, last_tile):
        pl.semaphore_signal(barrier, inc=1, device_id=other, device_id_type=MESH)
    pl.semaphore_wait(barrier, 40)

    to_next = pltpu.make_async_remote_copy(
        src_ref=noise_ref.at[pl.ds(24, 8)], dst_ref=extended.at[pl.ds(0, 8)], send_sem=halo_send.at[0],
        recv_sem=halo_recv.at[0], device_id=next_tile, device_id_type=MESH)
    to_last = pltpu.make_async_remote_copy(
        src_ref=noise_ref.at[pl.ds(0, 8)], dst_ref=extended.at[pl.ds(40, 8)], send_sem=halo_send.at[1],
        recv_sem=halo_recv.at[1], device_id=last_tile, device_id_type=MESH)

    @pl.when(s < 31)
    def _():
        to_next.start()

    @pl.when(s > 0)
    def _():
        to_last.start()

    own_load.wait()

    def send(rows, tile, send_sem, recv_sem, device):
        region = tiles.at[tile, rows]
        return pltpu.make_async_remote_copy(
            src_ref=region, dst_ref=region, send_sem=send_sem, recv_sem=recv_sem,
            device_id=device, device_id_type=MESH)

    classes = []
    start = 0
    for size, along_z_first, long_up in ((PA, True, True), (PB, True, False), (QA, False, True), (QB, False, False)):
        classes.append((pl.ds(start, size), along_z_first, long_up, False))
        start += size
    shared_base = start
    if RX:
        classes.append((pl.ds(pl.multiple_of(shared_base + x * RX, 16), RX), True, True, True))
    half = RX // 2

    def piece(owner, first, size):
        return pl.ds(pl.multiple_of(shared_base + owner * RX + first, 16), size)

    def placed(dy, i):
        dz = lax.rem(lax.div(i + 1, 2) * (2 * lax.rem(i, 2) - 1) + 8, 8)
        tile = lax.rem(y - dy + 4, 4) * 8 + lax.rem(z - dz + 8, 8)
        return tile, dy, dz

    def tile_of(n):
        part = lax.div(n, 8)
        middle = lax.rem(lax.div(part + 1, 2), 2)
        dy = middle * (1 + 2 * lax.rem(n, 2)) + 2 * lax.div(part, 3)
        return placed(dy, middle * lax.div(n - 8, 2) + (1 - middle) * lax.rem(n, 8))

    def across_of(n):
        col = lax.rem(n, 4)
        return placed(col + lax.div(col, 2) * (1 - 2 * lax.rem(col, 2)), lax.div(n, 4))

    def forward(n, chosen):
        for k in chosen:
            rows, along_z_first, long_up, shared = classes[k]
            tile, dy, dz = tile_of(n) if along_z_first else across_of(n)
            hi_z, hi_y = (4, 2) if long_up else (3, 1)

            @pl.when(n > 0)
            def _():
                send(rows, tile, tree_send.at[k], tree_recv.at[k, tile], sibling).wait_recv()

            go_zu = jnp.logical_or(dz == 0, jnp.logical_and(dz >= 1, dz < hi_z))
            go_zd = jnp.logical_or(dz == 0, dz > hi_z + 1)
            go_yu = jnp.logical_or(dy == 0, jnp.logical_and(dy >= 1, dy < hi_y))
            go_yd = jnp.logical_or(dy == 0, dy > hi_y + 1)
            if along_z_first:
                go_zu, go_zd = jnp.logical_and(go_zu, dy == 0), jnp.logical_and(go_zd, dy == 0)
            else:
                go_yu, go_yd = jnp.logical_and(go_yu, dz == 0), jnp.logical_and(go_yd, dz == 0)
            for go, device in ((go_zu, z_up), (go_zd, z_down), (go_yu, y_up), (go_yd, y_down)):
                @pl.when(go)
                def _():
                    send(rows, tile, tree_send.at[k], tree_recv.at[k, tile], device).start()
            if shared:
                @pl.when(n > 0)
                def _():
                    send(rows, tile, cross_send.at[0], cross_recv.at[0, tile], x_up).start()
                    send(rows, tile, cross_send.at[1], cross_recv.at[1, tile], x_down).start()

    def send_half(tile, device):
        region = halves.at[tile]
        return pltpu.make_async_remote_copy(
            src_ref=region, dst_ref=region, send_sem=half_send, recv_sem=half_recv.at[tile],
            device_id=device, device_id_type=MESH)

    def forward_half(n):
        tile, dy, dz = tile_of(n)

        @pl.when(n > 0)
        def _():
            send_half(tile, sibling).wait_recv()

        for go, device in ((jnp.logical_and(dy == 0, dz < 4), z_up),
                           (jnp.logical_and(dy == 0, jnp.logical_or(dz == 0, dz > 5)), z_down),
                           (dy < 2, y_up), (dy == 0, y_down)):
            @pl.when(go)
            def _():
                send_half(tile, device).start()

    def pass_on(n):
        tile, _, _ = tile_of(n)
        below, above = lax.rem(x + 3, 4), lax.rem(x + 1, 4)
        send(piece(below, 0, RX), tile, cross_send.at[0], cross_recv.at[0, tile], sibling).wait_recv()
        send(piece(below, 0, half), tile, cross_send.at[2], cross_recv.at[2, tile], x_up).start()
        send(piece(above, 0, RX), tile, cross_send.at[1], cross_recv.at[1, tile], sibling).wait_recv()
        send(piece(above, half, half), tile, cross_send.at[3], cross_recv.at[3, tile], x_down).start()

    def blocks_of(tile):
        return (tab_own[0, tile * 2], tab_own[0, tile * 2 + 1]), (tab_sib[0, tile * 2], tab_sib[0, tile * 2 + 1])

    def accumulate(tile, begin, end):
        (own_a, own_b), (sib_a, sib_b) = blocks_of(tile)
        total = accum[tile]
        for k in range(begin, end, 384):
            ks = pl.ds(k, min(384, end - k))
            lhs = jnp.concatenate(
                [own_f[own_a, :, ks], own_f[own_b, :, ks], sib_f[sib_a, :, ks], sib_f[sib_b, :, ks]], axis=0)
            total += jnp.dot(lhs, tiles[tile, ks, :], preferred_element_type=jnp.float32)
        accum[tile] = total

    def finish_tile(tile, carry):
        total = (accum[tile] * JAC_SCALE).astype(jnp.bfloat16)
        rows = pl.ds(pl.multiple_of(tile * 64, 64), 64)
        jac[c, rows, :] = total[:64]
        jac_out[rows, :] = total[64:]
        return carry

    def multiply(n):
        tile, _, _ = tile_of(n)
        if RX:
            far = lax.rem(x + 2, 4)

            @pl.when(n > 0)
            def _():
                send(piece(far, 0, half), tile, cross_send.at[2], cross_recv.at[2, tile], sibling).wait_recv()
                send(piece(far, half, half), tile, cross_send.at[3], cross_recv.at[3, tile], sibling).wait_recv()
        (own_a, own_b), _ = blocks_of(tile)
        accumulate(tile, 0, PA + PB)
        accumulate(tile, PA + PB + QA + QB, 4096)
        values = halves[tile].astype(jnp.float32)
        seen_a = jnp.zeros((32, 128), jnp.float32)
        seen_b = jnp.zeros((32, 128), jnp.float32)
        for k in range(32):
            ks = pl.ds(k * 128, 128)
            value = values[k:k + 1, :]
            seen_a += own_f[own_a, :, ks].astype(jnp.float32) * value
            seen_b += own_f[own_b, :, ks].astype(jnp.float32) * value
        rows = pl.ds(pl.multiple_of(tile * 64, 64), 64)
        accs[rows, :] = jnp.concatenate([seen_a, seen_b], axis=0)
        lane = lax.broadcasted_iota(jnp.int32, (32, 128), 1)
        gaps[rows, :] = jnp.concatenate(
            [jnp.where(lane == own_a, sound_t[...], 0.0) - seen_a,
             jnp.where(lane == own_b, sound_t[...], 0.0) - seen_b], axis=0)

    forward(0, (4, 0, 1, 2, 3))
    source, match = slot_tables(target_ref[...])
    tab_mine[...] = source
    tab_load = pltpu.make_async_copy(tab_mine, tab_own, load_sem.at[2])
    tab_load.start()
    tab_swap = pltpu.make_async_remote_copy(
        src_ref=tab_mine, dst_ref=tab_v, send_sem=pair_send.at[0], recv_sem=pair_recv.at[0],
        device_id=sibling, device_id_type=MESH)
    tab_swap.start()
    square[...] = jnp.zeros(square.shape, jnp.float32)
    square[0:32, 0:32] = sound_ref[...].astype(jnp.float32)
    sound_t[...] = square[...].T[0:32, :]
    fp_swap = pltpu.make_async_remote_copy(
        src_ref=fp_ref.at[0], dst_ref=sib_f.at[pl.ds(0, count)], send_sem=pair_send.at[1],
        recv_sem=pair_recv.at[1], device_id=sibling, device_id_type=MESH)
    fp_swap.start()
    own_f[count] = jnp.zeros(own_f.shape[1:], own_f.dtype)
    sib_f[count] = jnp.zeros(sib_f.shape[1:], sib_f.dtype)
    columns, (band_even, band_up, band_down) = smoothing_matrices()
    extended[8:40, :] = noise_ref[...]

    @pl.when(s > 0)
    def _():
        to_next.wait_recv()

    @pl.when(s == 0)
    def _():
        extended[0:8, :] = jnp.zeros((8, 128), jnp.float32)

    @pl.when(s < 31)
    def _():
        to_last.wait_recv()

    @pl.when(s == 31)
    def _():
        extended[40:48, :] = jnp.zeros((8, 128), jnp.float32)

    def exact(p, q):
        return jnp.dot(p, q, precision=HIGHEST, preferred_element_type=jnp.float32)

    mixed = exact(extended[...], columns)
    swapped = jnp.concatenate([mixed[:, 64:], mixed[:, :64]], axis=1)
    lane = lax.broadcasted_iota(jnp.int32, (32, 128), 1)
    smooth = exact(band_even, mixed) + jnp.where(
        lane < 64, exact(band_up, swapped), exact(band_down, swapped))
    proposal = KEEP * flux_ref[...] + BETA * prior_ref[...] * smooth
    proposal_ref[...] = proposal
    halves[s] = proposal.astype(jnp.bfloat16)
    forward_half(0)
    tab_swap.wait()
    sib_load = pltpu.make_async_copy(tab_v, tab_sib, load_sem.at[3])
    sib_load.start()
    tab_load.wait()
    sib_load.wait()

    def stream(n, ahead, limit, item):
        @pl.when(n <= ahead)
        def _():
            item(2 * n - 1)
            item(2 * n)

        @pl.when(jnp.logical_and(n > ahead, n + ahead < limit))
        def _():
            item(n + ahead)

    def cross_item(m):
        @pl.when(m < 32)
        def _():
            forward(m, (4,))

        @pl.when(m > LAG_CROSS)
        def _():
            pass_on(m - LAG_CROSS)

    def step(n, carry):
        stream(n, AHEAD_SHARED, 32 + LAG_CROSS, cross_item)

        @pl.when(n < 32)
        def _():
            forward(n, (0, 1))
            forward_half(n)
        stream(n, AHEAD_ACROSS, 32, lambda m: forward(m, (2, 3)))

        @pl.when(n == LAG_WORK)
        def _():
            fp_load.wait()
            fp_swap.wait()

        @pl.when(n >= LAG_WORK)
        def _():
            multiply(n - LAG_WORK)
            accumulate(across_of(n - LAG_WORK)[0], PA + PB, PA + PB + QA + QB)
        return carry

    accum[...] = jnp.zeros(accum.shape, jnp.float32)
    lax.fori_loop(1, 32 + LAG_WORK, step, 0)
    lax.fori_loop(0, 32, finish_tile, 0)
    whole = pltpu.make_async_remote_copy(
        src_ref=jac_out, dst_ref=jac.at[c], send_sem=jac_send, recv_sem=jac_recv,
        device_id=sibling, device_id_type=MESH)
    whole.start()
    mis = lax.dot_general(jnp.ones((8, 128), jnp.float32), gaps[...], (((1,), (1,)), ((), ())),
                          precision=HIGHEST, preferred_element_type=jnp.float32)

    for k, (rows, _, _, _) in enumerate(classes):
        region = tiles.at[pl.ds(0, 31), rows]
        pltpu.make_async_copy(region, region, tree_send.at[k]).wait()
    if RX:
        for k, size in enumerate((RX, RX, half, half)):
            region = tiles.at[pl.ds(0, 31), pl.ds(0, size)]
            pltpu.make_async_copy(region, region, cross_send.at[k]).wait()
    whole.wait()
    region = halves.at[pl.ds(0, 31)]
    pltpu.make_async_copy(region, region, half_send).wait()

    @pl.when(s < 31)
    def _():
        to_next.wait_send()

    @pl.when(s > 0)
    def _():
        to_last.wait_send()

    low, high = jac[0], jac[1]

    def gram(a, b):
        return lax.dot_general(a, b, (((0,), (0,)), ((), ())), preferred_element_type=jnp.float32)

    aug[0:128, :] = gram(low, low)
    aug[128:256, :] = gram(low, high)
    aug[256:384, :] = gram(high, high)
    mis_a = mis.astype(jnp.bfloat16)
    rest = mis - mis_a.astype(jnp.float32)
    mis_b = rest.astype(jnp.bfloat16)
    mis_c = (rest - mis_b.astype(jnp.float32)).astype(jnp.bfloat16)
    aug[384:, :] = jnp.zeros((128, 128), jnp.float32)
    for k, side in enumerate((low, high)):
        part = sum(jnp.dot(m, side, preferred_element_type=jnp.float32) for m in (mis_c, mis_b, mis_a))
        aug[384 + 8 * k:392 + 8 * k, :] = part

    def rows(index):
        return pl.ds(pl.multiple_of(index * 16, 16), 16)

    def scatter(k, carry):
        other, device = in_a(k)
        pltpu.make_async_remote_copy(
            src_ref=aug.at[rows(other)], dst_ref=parts.at[k - 1], send_sem=send_a, recv_sem=recv_a,
            device_id=device, device_id_type=MESH).start()
        return carry

    lax.fori_loop(1, 32, scatter, 0)

    def settle(region, send_sem, recv_sem):
        pltpu.make_async_copy(region, region, send_sem).wait()
        pltpu.make_async_copy(region, region, recv_sem).wait()

    seen = jnp.sum(accs[...].reshape(64, 32, 128), axis=-1)
    predicted_ref[...] = exact(match[:, :64], seen)
    settle(parts, send_a, recv_a)
    own = aug[rows(a), :]
    for k in range(31):
        own = own + parts[k]
    sums[b] = own

    def exchange(k, carry):
        _, device = in_b(k)
        pltpu.make_async_remote_copy(
            src_ref=sums.at[b], dst_ref=sums.at[b], send_sem=send_b, recv_sem=recv_b,
            device_id=device, device_id_type=MESH).start()
        return carry

    lax.fori_loop(1, 8, exchange, 0)
    settle(parts.at[pl.ds(0, 7)], send_b, recv_b)
    total = sums[0]
    for k in range(1, 8):
        total = total + sums[k]
    full[rows(a), :] = total

    def spread(k, carry):
        _, device = in_a(k)
        pltpu.make_async_remote_copy(
            src_ref=full.at[rows(a)], dst_ref=full.at[rows(a)], send_sem=send_c, recv_sem=recv_c,
            device_id=device, device_id_type=MESH).start()
        return carry

    lax.fori_loop(1, 32, spread, 0)
    settle(parts, send_c, recv_c)


def factor_kernel(full, proposal_in, predicted_in, proposal_ref, predicted_ref, u_ref, v_ref, work, solved):
    proposal_ref[...] = proposal_in[...]
    predicted_ref[...] = predicted_in[...]
    square = (128, 128)
    eye = (lax.broadcasted_iota(jnp.int32, square, 0) == lax.broadcasted_iota(jnp.int32, square, 1))
    eye = eye.astype(jnp.float32)
    rhs = full[384:512, :].T
    work[0:128, 0:128] = full[0:128, :] + eye
    work[0:128, 128:256] = full[128:256, :]
    work[128:256, 128:256] = full[256:384, :] + eye
    work[0:128, 256:384] = rhs
    work[128:256, 256:384] = jnp.concatenate([rhs[:, 8:], rhs[:, :8]], axis=1)
    factor_rows(work, u_ref, solved)
    v_ref[:, 0:128] = solved[0:128, :].T[0:1, :]
    v_ref[:, 128:256] = solved[128:256, :].T[0:1, :]


def whole_step(flux, noise, prior, target, sound, footprints, basis):
    vm = pl.BlockSpec(memory_space=pltpu.VMEM)
    hbm = pl.BlockSpec(memory_space=pl.ANY)
    dma = pltpu.SemaphoreType.DMA
    f32, bf16, i32 = jnp.float32, jnp.bfloat16, jnp.int32
    shapes = (jax.ShapeDtypeStruct((32, 128), f32), jax.ShapeDtypeStruct((32, 32), f32))
    proposal, predicted, summed = pl.pallas_call(
        step_kernel,
        out_shape=shapes + (jax.ShapeDtypeStruct((512, 128), f32),),
        in_specs=[vm, vm, vm, vm, vm, hbm, hbm],
        out_specs=(vm, vm, vm),
        scratch_shapes=[
            pltpu.VMEM((33, 32, 4096), bf16), pltpu.VMEM((33, 32, 4096), bf16),
            pltpu.VMEM((32, 4096, 128), bf16), pltpu.VMEM((32, 32, 128), bf16),
            pltpu.VMEM((2, 2048, 128), bf16), pltpu.VMEM((2048, 128), bf16),
            pltpu.VMEM((2048, 128), f32), pltpu.VMEM((2048, 128), f32), pltpu.VMEM((48, 128), f32),
            pltpu.VMEM((128, 128), f32), pltpu.VMEM((32, 128), f32),
            pltpu.VMEM((1, 128), i32), pltpu.VMEM((1, 128), i32), pltpu.SMEM((1, 128), i32), pltpu.SMEM((1, 128), i32),
            pltpu.VMEM((512, 128), f32), pltpu.VMEM((31, 16, 128), f32), pltpu.VMEM((8, 16, 128), f32), pltpu.VMEM((32, 128, 128), f32),
            dma((4,)), dma((2,)), dma((2,)), dma((5, 32)), dma((4, 32)), dma((5,)), dma((4,)),
            dma, dma, dma, dma((32,)), dma((2,)), dma((2,)),
            dma, dma, dma, dma, dma, dma,
        ],
        compiler_params=pltpu.CompilerParams(
            collective_id=0, has_side_effects=True, vmem_limit_bytes=60 * 1024 * 1024),
        name="assimilate",
    )(flux, noise, prior, target, sound, footprints, basis)
    return pl.pallas_call(
        factor_kernel,
        out_shape=shapes + (jax.ShapeDtypeStruct((256, 256), f32), jax.ShapeDtypeStruct((1, 256), f32)),
        in_specs=[vm, vm, vm],
        out_specs=(vm, vm, vm, vm),
        scratch_shapes=[pltpu.VMEM((256, 384), f32), pltpu.VMEM((256, 128), f32)],
        name="factor",
    )(summed, proposal, predicted)


def per_device(flux, noise, prior_scale, footprints, soundings, targets, basis):
    proposal, predicted, factor_up, rhs_value = whole_step(
        flux.reshape(32, 128), noise.reshape(32, 128), prior_scale.reshape(32, 128),
        targets.reshape(1, 32), soundings.reshape(32, 32), footprints, basis)
    return (proposal.reshape(1, 4096), predicted[None], factor_up, rhs_value.reshape(256))


def solution(mesh):
    return jax.shard_map(
        per_device,
        mesh=mesh,
        in_specs=(
            P("tm", "space"),
            P("tm", "space"),
            P("space"),
            P("tm", "space", None, None),
            P("tm", "space", None),
            P("tm", "space", None),
            P("space", None),
        ),
        out_specs=(P("tm", "space"), P("tm", "space", None), P(), P()),
        check_vma=False,
    )
```

```python
import math

import jax
import jax.numpy as jnp
from jax import lax
from jax.experimental import pallas as pl
from jax.experimental.pallas import tpu as pltpu
from jax.sharding import PartitionSpec as P

MESH = pl.DeviceIdType.MESH
HIGHEST = lax.Precision.HIGHEST
BLOCKS_HERE = 32
JAC_SCALE = float(262144) ** (-0.5)
REACH = 8
BETA = 0.6
KEEP = 0.8


def kernel_weights(reach):
    profile = [(1.0 + 2.0 * abs(d) / reach) * math.exp(-2.0 * abs(d) / reach) for d in range(-reach, reach + 1)]
    norm = math.sqrt(sum(p * p for p in profile))
    return [p / norm for p in profile]


KERNEL = kernel_weights(REACH)


def factor_rows(work, out_u, out_v):
    row = lax.broadcasted_iota(jnp.int32, (32, 128), 0)
    lane = lax.broadcasted_iota(jnp.int32, (32, 128), 1)
    wide_row = lax.broadcasted_iota(jnp.int32, (32, 256), 0)
    wide_lane = lax.broadcasted_iota(jnp.int32, (32, 256), 1)
    for k in range(8):
        k0, c0 = 32 * k, 128 * (k // 4)
        off = k0 - c0
        eye0 = (off + 64) % 128
        rows = work[k0:k0 + 32, :]
        e = jnp.where(jnp.logical_and(lane >= off, lane < off + 32), rows[:, c0:c0 + 128], 0.0)
        e = e + (lane - eye0 == row).astype(jnp.float32)
        for j in range(0, 32, 8):
            cols = [jnp.broadcast_to(e[:, off + p:off + p + 1], (32, 128)) for p in range(j, j + 8)]
            heads = [e[p:p + 1, :] for p in range(j, j + 8)]
            for i in range(8):
                p = j + i
                scale = 1.0 / cols[i][p:p + 1, :]
                below = jnp.where(row > p, cols[i], 0.0)
                scaled = heads[i] * scale
                for l in range(i + 1, 8):
                    heads[l] = heads[l] - cols[i][j + l:j + l + 1, :] * scaled
                    cols[l] = cols[l] - below * (cols[l][p:p + 1, :] * scale)
                e = e - below * scaled
        diagonal = jnp.sum(jnp.where(lane == row + off, e, 0.0), axis=1, keepdims=True)
        e = e * lax.rsqrt(diagonal)
        inverse = e[:, eye0:eye0 + 32]
        panel = jnp.dot(inverse, rows[:, c0:], preferred_element_type=jnp.float32, precision=HIGHEST)
        upper = panel[:, :256 - c0]
        if c0:
            upper = jnp.concatenate([jnp.zeros((32, c0), jnp.float32), upper], axis=1)
        upper = jnp.where(wide_lane >= wide_row + k0, upper, 0.0)
        out_u[k0:k0 + 32, :] = upper
        out_v[k0:k0 + 32, :] = panel[:, 256 - c0:]
        if k < 7:
            k1 = k0 + 32
            c1 = 128 * (k1 // 128)
            left = panel[:, c1 - c0:256 - c0]
            update = lax.dot_general(left, panel[:, c1 - c0:], (((0,), (0,)), ((), ())),
                                     preferred_element_type=jnp.float32, precision=HIGHEST)
            work[k1:, c1:] = work[k1:, c1:] - update[k1 - c1:]


PA, PB, QA, QB = 352, 928, 576, 448
RX = 448
AHEAD = 11
LAG_CROSS, LAG_WORK = 5, 2


def weight(position):
    return KERNEL[REACH + position]


def slot_tables(target):
    row = lax.broadcasted_iota(jnp.int32, (32, 32), 0)
    lane = lax.broadcasted_iota(jnp.int32, (32, 32), 1)
    across = jnp.broadcast_to(target, (32, 32))
    down = jnp.sum(jnp.where(row == lane, across, 0), axis=1, keepdims=True)
    earlier = jnp.logical_and(across == down, lane < row)
    slot = 2 * down + jnp.sum(jnp.where(earlier, 1, 0), axis=1, keepdims=True)
    slots = lax.broadcasted_iota(jnp.int32, (32, 128), 1)
    block = lax.broadcasted_iota(jnp.int32, (32, 128), 0)
    match = slot == slots
    source = 32 + jnp.sum(jnp.where(match, block - 32, 0), axis=0, keepdims=True)
    return source, jnp.where(match, 1.0, 0.0)


def smoothing_matrices():
    lane = lax.broadcasted_iota(jnp.int32, (128, 128), 1)
    source = lax.broadcasted_iota(jnp.int32, (128, 128), 0)
    same = lax.div(lane, 64) == lax.div(source, 64)
    gap = lax.rem(source - lane + 64 + REACH, 64)
    columns = jnp.zeros((128, 128), jnp.float32)
    for b in range(-REACH, REACH + 1):
        columns = columns + jnp.where(jnp.logical_and(same, gap == b + REACH), weight(b), 0.0)
    row = lax.broadcasted_iota(jnp.int32, (32, 48), 0)
    shift = lax.broadcasted_iota(jnp.int32, (32, 48), 1) - 8 - row
    bands = []
    for offset in (0, 1, -1):
        band = jnp.zeros((32, 48), jnp.float32)
        for d in range(-4, 5):
            if abs(2 * d + offset) <= REACH:
                band = band + jnp.where(shift == d, weight(2 * d + offset), 0.0)
        bands.append(band)
    return columns, bands


def step_kernel(flux_ref, noise_ref, prior_ref, target_ref, sound_ref, fp_ref, basis_ref,
                proposal_ref, predicted_ref, full,
                own_f, sib_f, tiles, halves, jac, jac_out, accs, gaps, extended, square, sound_t,
                tab_mine, tab_v, tab_own, tab_sib, aug, parts, sums, accum,
                load_sem, pair_send, pair_recv, tree_recv, cross_recv, tree_send, cross_send,
                jac_send, jac_recv, half_send, half_recv, halo_send, halo_recv,
                send_a, recv_a, send_b, recv_b, send_c, recv_c):
    t = lax.axis_index("tm")
    s = lax.axis_index("space")
    x, c = lax.div(t, 2), lax.rem(t, 2)
    y, z = lax.div(s, 8), lax.rem(s, 8)
    sibling = (x * 2 + (1 - c), s)
    z_up = (t, y * 8 + lax.rem(z + 1, 8))
    z_down = (t, y * 8 + lax.rem(z + 7, 8))
    y_up = (t, lax.rem(y + 1, 4) * 8 + z)
    y_down = (t, lax.rem(y + 3, 4) * 8 + z)
    x_up = (lax.rem(x + 1, 4) * 2 + c, s)
    x_down = (lax.rem(x + 3, 4) * 2 + c, s)
    count = BLOCKS_HERE

    own_load = pltpu.make_async_copy(
        basis_ref.at[:, pl.ds(pl.multiple_of(c * 128, 128), 128)], tiles.at[s], load_sem.at[0])
    own_load.start()
    fp_load = pltpu.make_async_copy(fp_ref.at[0], own_f.at[pl.ds(0, count)], load_sem.at[1])
    fp_load.start()

    a = t * 4 + y
    b = z

    def in_a(k):
        other = lax.rem(a + k, 32)
        return other, (lax.div(other, 4), lax.rem(other, 4) * 8 + z)

    def in_b(k):
        other = lax.rem(b + k, 8)
        return other, (t, y * 8 + other)

    next_tile = (t, lax.rem(s + 1, 32))
    last_tile = (t, lax.rem(s + 31, 32))
    barrier = pltpu.get_barrier_semaphore()

    def greet_a(k, carry):
        pl.semaphore_signal(barrier, inc=1, device_id=in_a(k)[1], device_id_type=MESH)
        return carry

    def greet_b(k, carry):
        pl.semaphore_signal(barrier, inc=1, device_id=in_b(k)[1], device_id_type=MESH)
        return carry

    lax.fori_loop(1, 32, greet_a, 0)
    lax.fori_loop(1, 8, greet_b, 0)
    for other in (next_tile, last_tile):
        pl.semaphore_signal(barrier, inc=1, device_id=other, device_id_type=MESH)
    pl.semaphore_wait(barrier, 40)

    to_next = pltpu.make_async_remote_copy(
        src_ref=noise_ref.at[pl.ds(24, 8)], dst_ref=extended.at[pl.ds(0, 8)], send_sem=halo_send.at[0],
        recv_sem=halo_recv.at[0], device_id=next_tile, device_id_type=MESH)
    to_last = pltpu.make_async_remote_copy(
        src_ref=noise_ref.at[pl.ds(0, 8)], dst_ref=extended.at[pl.ds(40, 8)], send_sem=halo_send.at[1],
        recv_sem=halo_recv.at[1], device_id=last_tile, device_id_type=MESH)

    @pl.when(s < 31)
    def _():
        to_next.start()

    @pl.when(s > 0)
    def _():
        to_last.start()

    own_load.wait()

    def send(rows, tile, send_sem, recv_sem, device):
        region = tiles.at[tile, rows]
        return pltpu.make_async_remote_copy(
            src_ref=region, dst_ref=region, send_sem=send_sem, recv_sem=recv_sem,
            device_id=device, device_id_type=MESH)

    classes = []
    start = 0
    for size, along_z_first, long_up in ((PA, True, True), (PB, True, False), (QA, False, True), (QB, False, False)):
        classes.append((pl.ds(start, size), along_z_first, long_up, False))
        start += size
    shared_base = start
    if RX:
        classes.append((pl.ds(pl.multiple_of(shared_base + x * RX, 16), RX), True, True, True))
    half = RX // 2

    def piece(owner, first, size):
        return pl.ds(pl.multiple_of(shared_base + owner * RX + first, 16), size)

    def placed(dy, i):
        dz = lax.rem(lax.div(i + 1, 2) * (2 * lax.rem(i, 2) - 1) + 8, 8)
        tile = lax.rem(y - dy + 4, 4) * 8 + lax.rem(z - dz + 8, 8)
        return tile, dy, dz

    def tile_of(n):
        part = lax.div(n, 8)
        middle = lax.rem(lax.div(part + 1, 2), 2)
        dy = middle * (1 + 2 * lax.rem(n, 2)) + 2 * lax.div(part, 3)
        return placed(dy, middle * lax.div(n - 8, 2) + (1 - middle) * lax.rem(n, 8))

    def across_of(n):
        col = lax.rem(n, 4)
        return placed(col + lax.div(col, 2) * (1 - 2 * lax.rem(col, 2)), lax.div(n, 4))

    def forward(n, chosen):
        for k in chosen:
            rows, along_z_first, long_up, shared = classes[k]
            tile, dy, dz = tile_of(n) if along_z_first else across_of(n)
            hi_z, hi_y = (4, 2) if long_up else (3, 1)

            @pl.when(n > 0)
            def _():
                send(rows, tile, tree_send.at[k], tree_recv.at[k, tile], sibling).wait_recv()

            go_zu = jnp.logical_or(dz == 0, jnp.logical_and(dz >= 1, dz < hi_z))
            go_zd = jnp.logical_or(dz == 0, dz > hi_z + 1)
            go_yu = jnp.logical_or(dy == 0, jnp.logical_and(dy >= 1, dy < hi_y))
            go_yd = jnp.logical_or(dy == 0, dy > hi_y + 1)
            if along_z_first:
                go_zu, go_zd = jnp.logical_and(go_zu, dy == 0), jnp.logical_and(go_zd, dy == 0)
            else:
                go_yu, go_yd = jnp.logical_and(go_yu, dz == 0), jnp.logical_and(go_yd, dz == 0)
            for go, device in ((go_zu, z_up), (go_zd, z_down), (go_yu, y_up), (go_yd, y_down)):
                @pl.when(go)
                def _():
                    send(rows, tile, tree_send.at[k], tree_recv.at[k, tile], device).start()
            if shared:
                @pl.when(n > 0)
                def _():
                    send(rows, tile, cross_send.at[0], cross_recv.at[0, tile], x_up).start()
                    send(rows, tile, cross_send.at[1], cross_recv.at[1, tile], x_down).start()

    def send_half(tile, device):
        region = halves.at[tile]
        return pltpu.make_async_remote_copy(
            src_ref=region, dst_ref=region, send_sem=half_send, recv_sem=half_recv.at[tile],
            device_id=device, device_id_type=MESH)

    def forward_half(n):
        tile, dy, dz = tile_of(n)

        @pl.when(n > 0)
        def _():
            send_half(tile, sibling).wait_recv()

        for go, device in ((jnp.logical_and(dy == 0, dz < 4), z_up),
                           (jnp.logical_and(dy == 0, jnp.logical_or(dz == 0, dz > 5)), z_down),
                           (dy < 2, y_up), (dy == 0, y_down)):
            @pl.when(go)
            def _():
                send_half(tile, device).start()

    def pass_on(n):
        tile, _, _ = tile_of(n)
        below, above = lax.rem(x + 3, 4), lax.rem(x + 1, 4)
        send(piece(below, 0, RX), tile, cross_send.at[0], cross_recv.at[0, tile], sibling).wait_recv()
        send(piece(below, 0, half), tile, cross_send.at[2], cross_recv.at[2, tile], x_up).start()
        send(piece(above, 0, RX), tile, cross_send.at[1], cross_recv.at[1, tile], sibling).wait_recv()
        send(piece(above, half, half), tile, cross_send.at[3], cross_recv.at[3, tile], x_down).start()

    def blocks_of(tile):
        return (tab_own[0, tile * 2], tab_own[0, tile * 2 + 1]), (tab_sib[0, tile * 2], tab_sib[0, tile * 2 + 1])

    def accumulate(tile, begin, end):
        (own_a, own_b), (sib_a, sib_b) = blocks_of(tile)
        total = accum[tile]
        for k in range(begin, end, 384):
            ks = pl.ds(k, min(384, end - k))
            lhs = jnp.concatenate(
                [own_f[own_a, :, ks], own_f[own_b, :, ks], sib_f[sib_a, :, ks], sib_f[sib_b, :, ks]], axis=0)
            total += jnp.dot(lhs, tiles[tile, ks, :], preferred_element_type=jnp.float32)
        accum[tile] = total

    def finish_tile(tile, carry):
        total = (accum[tile] * JAC_SCALE).astype(jnp.bfloat16)
        rows = pl.ds(pl.multiple_of(tile * 64, 64), 64)
        jac[c, rows, :] = total[:64]
        jac_out[rows, :] = total[64:]
        return carry

    def multiply(n):
        tile, _, _ = tile_of(n)
        if RX:
            far = lax.rem(x + 2, 4)

            @pl.when(n > 0)
            def _():
                send(piece(far, 0, half), tile, cross_send.at[2], cross_recv.at[2, tile], sibling).wait_recv()
                send(piece(far, half, half), tile, cross_send.at[3], cross_recv.at[3, tile], sibling).wait_recv()
        (own_a, own_b), _ = blocks_of(tile)
        accumulate(tile, 0, PA + PB)
        accumulate(tile, PA + PB + QA + QB, 4096)
        values = halves[tile].astype(jnp.float32)
        seen_a = jnp.zeros((32, 128), jnp.float32)
        seen_b = jnp.zeros((32, 128), jnp.float32)
        for k in range(32):
            ks = pl.ds(k * 128, 128)
            value = values[k:k + 1, :]
            seen_a += own_f[own_a, :, ks].astype(jnp.float32) * value
            seen_b += own_f[own_b, :, ks].astype(jnp.float32) * value
        rows = pl.ds(pl.multiple_of(tile * 64, 64), 64)
        accs[rows, :] = jnp.concatenate([seen_a, seen_b], axis=0)
        lane = lax.broadcasted_iota(jnp.int32, (32, 128), 1)
        gaps[rows, :] = jnp.concatenate(
            [jnp.where(lane == own_a, sound_t[...], 0.0) - seen_a,
             jnp.where(lane == own_b, sound_t[...], 0.0) - seen_b], axis=0)

    forward(0, (4, 0, 2))
    source, match = slot_tables(target_ref[...])
    tab_mine[...] = source
    tab_load = pltpu.make_async_copy(tab_mine, tab_own, load_sem.at[2])
    tab_load.start()
    tab_swap = pltpu.make_async_remote_copy(
        src_ref=tab_mine, dst_ref=tab_v, send_sem=pair_send.at[0], recv_sem=pair_recv.at[0],
        device_id=sibling, device_id_type=MESH)
    tab_swap.start()
    square[...] = jnp.zeros(square.shape, jnp.float32)
    square[0:32, 0:32] = sound_ref[...].astype(jnp.float32)
    sound_t[...] = square[...].T[0:32, :]
    fp_swap = pltpu.make_async_remote_copy(
        src_ref=fp_ref.at[0], dst_ref=sib_f.at[pl.ds(0, count)], send_sem=pair_send.at[1],
        recv_sem=pair_recv.at[1], device_id=sibling, device_id_type=MESH)
    fp_swap.start()
    own_f[count] = jnp.zeros(own_f.shape[1:], own_f.dtype)
    sib_f[count] = jnp.zeros(sib_f.shape[1:], sib_f.dtype)
    columns, (band_even, band_up, band_down) = smoothing_matrices()
    extended[8:40, :] = noise_ref[...]

    @pl.when(s > 0)
    def _():
        to_next.wait_recv()

    @pl.when(s == 0)
    def _():
        extended[0:8, :] = jnp.zeros((8, 128), jnp.float32)

    @pl.when(s < 31)
    def _():
        to_last.wait_recv()

    @pl.when(s == 31)
    def _():
        extended[40:48, :] = jnp.zeros((8, 128), jnp.float32)

    def exact(p, q):
        return jnp.dot(p, q, precision=HIGHEST, preferred_element_type=jnp.float32)

    mixed = exact(extended[...], columns)
    swapped = jnp.concatenate([mixed[:, 64:], mixed[:, :64]], axis=1)
    lane = lax.broadcasted_iota(jnp.int32, (32, 128), 1)
    smooth = exact(band_even, mixed) + jnp.where(
        lane < 64, exact(band_up, swapped), exact(band_down, swapped))
    proposal = KEEP * flux_ref[...] + BETA * prior_ref[...] * smooth
    proposal_ref[...] = proposal
    halves[s] = proposal.astype(jnp.bfloat16)
    forward_half(0)
    tab_swap.wait()
    sib_load = pltpu.make_async_copy(tab_v, tab_sib, load_sem.at[3])
    sib_load.start()
    tab_load.wait()
    sib_load.wait()

    def cross_item(m):
        @pl.when(m < 32)
        def _():
            forward(m, (4,))

        @pl.when(m > LAG_CROSS)
        def _():
            pass_on(m - LAG_CROSS)

    def early_item(m, carry):
        cross_item(m)
        return carry

    def step(n, carry):
        @pl.when(n < 32)
        def _():
            forward(n, (2, 3))

        @pl.when(n + AHEAD < 32 + LAG_CROSS)
        def _():
            cross_item(n + AHEAD)

        @pl.when(n < 32)
        def _():
            forward(n, (0, 1))
            forward_half(n)

        @pl.when(n == LAG_WORK)
        def _():
            fp_load.wait()
            fp_swap.wait()

        @pl.when(n >= LAG_WORK)
        def _():
            multiply(n - LAG_WORK)
            accumulate(across_of(n - LAG_WORK)[0], PA + PB, PA + PB + QA + QB)
        return carry

    lax.fori_loop(1, 2, early_item, 0)
    forward(0, (3,))
    lax.fori_loop(2, 6, early_item, 0)
    forward(0, (1,))
    lax.fori_loop(6, 12, early_item, 0)
    accum[...] = jnp.zeros(accum.shape, jnp.float32)
    lax.fori_loop(1, 32 + LAG_WORK, step, 0)
    lax.fori_loop(0, 32, finish_tile, 0)
    whole = pltpu.make_async_remote_copy(
        src_ref=jac_out, dst_ref=jac.at[c], send_sem=jac_send, recv_sem=jac_recv,
        device_id=sibling, device_id_type=MESH)
    whole.start()
    mis = lax.dot_general(jnp.ones((8, 128), jnp.float32), gaps[...], (((1,), (1,)), ((), ())),
                          precision=HIGHEST, preferred_element_type=jnp.float32)

    for k, (rows, _, _, _) in enumerate(classes):
        region = tiles.at[pl.ds(0, 31), rows]
        pltpu.make_async_copy(region, region, tree_send.at[k]).wait()
    if RX:
        for k, size in enumerate((RX, RX, half, half)):
            region = tiles.at[pl.ds(0, 31), pl.ds(0, size)]
            pltpu.make_async_copy(region, region, cross_send.at[k]).wait()
    whole.wait()
    region = halves.at[pl.ds(0, 31)]
    pltpu.make_async_copy(region, region, half_send).wait()

    @pl.when(s < 31)
    def _():
        to_next.wait_send()

    @pl.when(s > 0)
    def _():
        to_last.wait_send()

    low, high = jac[0], jac[1]

    def gram(a, b):
        return lax.dot_general(a, b, (((0,), (0,)), ((), ())), preferred_element_type=jnp.float32)

    aug[0:128, :] = gram(low, low)
    aug[128:256, :] = gram(low, high)
    aug[256:384, :] = gram(high, high)
    mis_a = mis.astype(jnp.bfloat16)
    rest = mis - mis_a.astype(jnp.float32)
    mis_b = rest.astype(jnp.bfloat16)
    mis_c = (rest - mis_b.astype(jnp.float32)).astype(jnp.bfloat16)
    aug[384:, :] = jnp.zeros((128, 128), jnp.float32)
    for k, side in enumerate((low, high)):
        part = sum(jnp.dot(m, side, preferred_element_type=jnp.float32) for m in (mis_c, mis_b, mis_a))
        aug[384 + 8 * k:392 + 8 * k, :] = part

    def rows(index):
        return pl.ds(pl.multiple_of(index * 16, 16), 16)

    def scatter(k, carry):
        other, device = in_a(k)
        pltpu.make_async_remote_copy(
            src_ref=aug.at[rows(other)], dst_ref=parts.at[k - 1], send_sem=send_a, recv_sem=recv_a,
            device_id=device, device_id_type=MESH).start()
        return carry

    lax.fori_loop(1, 32, scatter, 0)

    def settle(region, send_sem, recv_sem):
        pltpu.make_async_copy(region, region, send_sem).wait()
        pltpu.make_async_copy(region, region, recv_sem).wait()

    seen = jnp.sum(accs[...].reshape(64, 32, 128), axis=-1)
    predicted_ref[...] = exact(match[:, :64], seen)
    settle(parts, send_a, recv_a)
    own = aug[rows(a), :]
    for k in range(31):
        own = own + parts[k]
    sums[b] = own

    def exchange(k, carry):
        _, device = in_b(k)
        pltpu.make_async_remote_copy(
            src_ref=sums.at[b], dst_ref=sums.at[b], send_sem=send_b, recv_sem=recv_b,
            device_id=device, device_id_type=MESH).start()
        return carry

    lax.fori_loop(1, 8, exchange, 0)
    settle(parts.at[pl.ds(0, 7)], send_b, recv_b)
    total = sums[0]
    for k in range(1, 8):
        total = total + sums[k]
    full[rows(a), :] = total

    def spread(k, carry):
        _, device = in_a(k)
        pltpu.make_async_remote_copy(
            src_ref=full.at[rows(a)], dst_ref=full.at[rows(a)], send_sem=send_c, recv_sem=recv_c,
            device_id=device, device_id_type=MESH).start()
        return carry

    lax.fori_loop(1, 32, spread, 0)
    settle(parts, send_c, recv_c)


def factor_kernel(full, proposal_in, predicted_in, proposal_ref, predicted_ref, u_ref, v_ref, work, solved):
    proposal_ref[...] = proposal_in[...]
    predicted_ref[...] = predicted_in[...]
    square = (128, 128)
    eye = (lax.broadcasted_iota(jnp.int32, square, 0) == lax.broadcasted_iota(jnp.int32, square, 1))
    eye = eye.astype(jnp.float32)
    rhs = full[384:512, :].T
    work[0:128, 0:128] = full[0:128, :] + eye
    work[0:128, 128:256] = full[128:256, :]
    work[128:256, 128:256] = full[256:384, :] + eye
    work[0:128, 256:384] = rhs
    work[128:256, 256:384] = jnp.concatenate([rhs[:, 8:], rhs[:, :8]], axis=1)
    factor_rows(work, u_ref, solved)
    v_ref[:, 0:128] = solved[0:128, :].T[0:1, :]
    v_ref[:, 128:256] = solved[128:256, :].T[0:1, :]


def whole_step(flux, noise, prior, target, sound, footprints, basis):
    vm = pl.BlockSpec(memory_space=pltpu.VMEM)
    hbm = pl.BlockSpec(memory_space=pl.ANY)
    dma = pltpu.SemaphoreType.DMA
    f32, bf16, i32 = jnp.float32, jnp.bfloat16, jnp.int32
    shapes = (jax.ShapeDtypeStruct((32, 128), f32), jax.ShapeDtypeStruct((32, 32), f32))
    proposal, predicted, summed = pl.pallas_call(
        step_kernel,
        out_shape=shapes + (jax.ShapeDtypeStruct((512, 128), f32),),
        in_specs=[vm, vm, vm, vm, vm, hbm, hbm],
        out_specs=(vm, vm, vm),
        scratch_shapes=[
            pltpu.VMEM((33, 32, 4096), bf16), pltpu.VMEM((33, 32, 4096), bf16),
            pltpu.VMEM((32, 4096, 128), bf16), pltpu.VMEM((32, 32, 128), bf16),
            pltpu.VMEM((2, 2048, 128), bf16), pltpu.VMEM((2048, 128), bf16),
            pltpu.VMEM((2048, 128), f32), pltpu.VMEM((2048, 128), f32), pltpu.VMEM((48, 128), f32),
            pltpu.VMEM((128, 128), f32), pltpu.VMEM((32, 128), f32),
            pltpu.VMEM((1, 128), i32), pltpu.VMEM((1, 128), i32), pltpu.SMEM((1, 128), i32), pltpu.SMEM((1, 128), i32),
            pltpu.VMEM((512, 128), f32), pltpu.VMEM((31, 16, 128), f32), pltpu.VMEM((8, 16, 128), f32), pltpu.VMEM((32, 128, 128), f32),
            dma((4,)), dma((2,)), dma((2,)), dma((5, 32)), dma((4, 32)), dma((5,)), dma((4,)),
            dma, dma, dma, dma((32,)), dma((2,)), dma((2,)),
            dma, dma, dma, dma, dma, dma,
        ],
        compiler_params=pltpu.CompilerParams(
            collective_id=0, has_side_effects=True, vmem_limit_bytes=60 * 1024 * 1024),
        name="assimilate",
    )(flux, noise, prior, target, sound, footprints, basis)
    return pl.pallas_call(
        factor_kernel,
        out_shape=shapes + (jax.ShapeDtypeStruct((256, 256), f32), jax.ShapeDtypeStruct((1, 256), f32)),
        in_specs=[vm, vm, vm],
        out_specs=(vm, vm, vm, vm),
        scratch_shapes=[pltpu.VMEM((256, 384), f32), pltpu.VMEM((256, 128), f32)],
        name="factor",
    )(summed, proposal, predicted)


def per_device(flux, noise, prior_scale, footprints, soundings, targets, basis):
    proposal, predicted, factor_up, rhs_value = whole_step(
        flux.reshape(32, 128), noise.reshape(32, 128), prior_scale.reshape(32, 128),
        targets.reshape(1, 32), soundings.reshape(32, 32), footprints, basis)
    return (proposal.reshape(1, 4096), predicted[None], factor_up, rhs_value.reshape(256))


def solution(mesh):
    return jax.shard_map(
        per_device,
        mesh=mesh,
        in_specs=(
            P("tm", "space"),
            P("tm", "space"),
            P("space"),
            P("tm", "space", None, None),
            P("tm", "space", None),
            P("tm", "space", None),
            P("space", None),
        ),
        out_specs=(P("tm", "space"), P("tm", "space", None), P(), P()),
        check_vma=False,
    )
```

```python
import math

import jax
import jax.numpy as jnp
from jax import lax
from jax.experimental import pallas as pl
from jax.experimental.pallas import tpu as pltpu
from jax.sharding import PartitionSpec as P

MESH = pl.DeviceIdType.MESH
HIGHEST = lax.Precision.HIGHEST
BLOCKS_HERE = 32
JAC_SCALE = float(262144) ** (-0.5)
REACH = 8
BETA = 0.6
KEEP = 0.8


def kernel_weights(reach):
    profile = [(1.0 + 2.0 * abs(d) / reach) * math.exp(-2.0 * abs(d) / reach) for d in range(-reach, reach + 1)]
    norm = math.sqrt(sum(p * p for p in profile))
    return [p / norm for p in profile]


KERNEL = kernel_weights(REACH)


def factor_rows(work, out_u, out_v):
    row = lax.broadcasted_iota(jnp.int32, (32, 128), 0)
    lane = lax.broadcasted_iota(jnp.int32, (32, 128), 1)
    wide_row = lax.broadcasted_iota(jnp.int32, (32, 256), 0)
    wide_lane = lax.broadcasted_iota(jnp.int32, (32, 256), 1)
    for k in range(8):
        k0, c0 = 32 * k, 128 * (k // 4)
        off = k0 - c0
        eye0 = (off + 64) % 128
        rows = work[k0:k0 + 32, :]
        e = jnp.where(jnp.logical_and(lane >= off, lane < off + 32), rows[:, c0:c0 + 128], 0.0)
        e = e + (lane - eye0 == row).astype(jnp.float32)
        for j in range(0, 32, 8):
            cols = [jnp.broadcast_to(e[:, off + p:off + p + 1], (32, 128)) for p in range(j, j + 8)]
            heads = [e[p:p + 1, :] for p in range(j, j + 8)]
            for i in range(8):
                p = j + i
                scale = 1.0 / cols[i][p:p + 1, :]
                below = jnp.where(row > p, cols[i], 0.0)
                scaled = heads[i] * scale
                for l in range(i + 1, 8):
                    heads[l] = heads[l] - cols[i][j + l:j + l + 1, :] * scaled
                    cols[l] = cols[l] - below * (cols[l][p:p + 1, :] * scale)
                e = e - below * scaled
        diagonal = jnp.sum(jnp.where(lane == row + off, e, 0.0), axis=1, keepdims=True)
        e = e * lax.rsqrt(diagonal)
        inverse = e[:, eye0:eye0 + 32]
        panel = jnp.dot(inverse, rows[:, c0:], preferred_element_type=jnp.float32, precision=HIGHEST)
        upper = panel[:, :256 - c0]
        if c0:
            upper = jnp.concatenate([jnp.zeros((32, c0), jnp.float32), upper], axis=1)
        upper = jnp.where(wide_lane >= wide_row + k0, upper, 0.0)
        out_u[k0:k0 + 32, :] = upper
        out_v[k0:k0 + 32, :] = panel[:, 256 - c0:]
        if k < 7:
            k1 = k0 + 32
            c1 = 128 * (k1 // 128)
            left = panel[:, c1 - c0:256 - c0]
            update = lax.dot_general(left, panel[:, c1 - c0:], (((0,), (0,)), ((), ())),
                                     preferred_element_type=jnp.float32, precision=HIGHEST)
            work[k1:, c1:] = work[k1:, c1:] - update[k1 - c1:]


PA, PB, QA, QB = 368, 912, 656, 368
RX = 448
AHEAD = 11
LAG_CROSS, LAG_WORK = 6, 2


def weight(position):
    return KERNEL[REACH + position]


def slot_tables(target):
    row = lax.broadcasted_iota(jnp.int32, (32, 32), 0)
    lane = lax.broadcasted_iota(jnp.int32, (32, 32), 1)
    across = jnp.broadcast_to(target, (32, 32))
    down = jnp.sum(jnp.where(row == lane, across, 0), axis=1, keepdims=True)
    earlier = jnp.logical_and(across == down, lane < row)
    slot = 2 * down + jnp.sum(jnp.where(earlier, 1, 0), axis=1, keepdims=True)
    slots = lax.broadcasted_iota(jnp.int32, (32, 128), 1)
    block = lax.broadcasted_iota(jnp.int32, (32, 128), 0)
    match = slot == slots
    source = 32 + jnp.sum(jnp.where(match, block - 32, 0), axis=0, keepdims=True)
    even = jnp.where(slot == 2 * lane, 1.0, 0.0)
    odd = jnp.where(slot == 2 * lane + 1, 1.0, 0.0)
    return source, even, odd


def smoothing_matrices():
    lane = lax.broadcasted_iota(jnp.int32, (128, 128), 1)
    source = lax.broadcasted_iota(jnp.int32, (128, 128), 0)
    same = lax.div(lane, 64) == lax.div(source, 64)
    gap = lax.rem(source - lane + 64 + REACH, 64)
    columns = jnp.zeros((128, 128), jnp.float32)
    for b in range(-REACH, REACH + 1):
        columns = columns + jnp.where(jnp.logical_and(same, gap == b + REACH), weight(b), 0.0)
    row = lax.broadcasted_iota(jnp.int32, (32, 48), 0)
    shift = lax.broadcasted_iota(jnp.int32, (32, 48), 1) - 8 - row
    bands = []
    for offset in (0, 1, -1):
        band = jnp.zeros((32, 48), jnp.float32)
        for d in range(-4, 5):
            if abs(2 * d + offset) <= REACH:
                band = band + jnp.where(shift == d, weight(2 * d + offset), 0.0)
        bands.append(band)
    return columns, bands


def step_kernel(flux_ref, noise_ref, prior_ref, target_ref, sound_ref, fp_ref, basis_ref,
                proposal_ref, predicted_ref, full,
                own_f, sib_f, tiles, halves, jac, jac_out, accs, gaps, extended, square, sound_t,
                tab_mine, tab_v, tab_own, tab_sib, aug, parts, sums, accum,
                load_sem, pair_send, pair_recv, tree_recv, cross_recv, tree_send, cross_send,
                jac_send, jac_recv, half_send, half_recv, halo_send, halo_recv,
                send_a, recv_a, send_b, recv_b, send_c, recv_c):
    t = lax.axis_index("tm")
    s = lax.axis_index("space")
    x, c = lax.div(t, 2), lax.rem(t, 2)
    y, z = lax.div(s, 8), lax.rem(s, 8)
    sibling = (x * 2 + (1 - c), s)
    z_up = (t, y * 8 + lax.rem(z + 1, 8))
    z_down = (t, y * 8 + lax.rem(z + 7, 8))
    y_up = (t, lax.rem(y + 1, 4) * 8 + z)
    y_down = (t, lax.rem(y + 3, 4) * 8 + z)
    x_up = (lax.rem(x + 1, 4) * 2 + c, s)
    x_down = (lax.rem(x + 3, 4) * 2 + c, s)
    count = BLOCKS_HERE

    own_load = pltpu.make_async_copy(
        basis_ref.at[:, pl.ds(pl.multiple_of(c * 128, 128), 128)], tiles.at[s], load_sem.at[0])
    own_load.start()
    fp_load = pltpu.make_async_copy(fp_ref.at[0], own_f.at[pl.ds(0, count)], load_sem.at[1])
    fp_load.start()

    a = t * 4 + y
    b = z

    def in_a(k):
        other = lax.rem(a + k, 32)
        return other, (lax.div(other, 4), lax.rem(other, 4) * 8 + z)

    def in_b(k):
        other = lax.rem(b + k, 8)
        return other, (t, y * 8 + other)

    next_tile = (t, lax.rem(s + 1, 32))
    last_tile = (t, lax.rem(s + 31, 32))
    barrier = pltpu.get_barrier_semaphore()

    def greet_a(k, carry):
        pl.semaphore_signal(barrier, inc=1, device_id=in_a(k)[1], device_id_type=MESH)
        return carry

    def greet_b(k, carry):
        pl.semaphore_signal(barrier, inc=1, device_id=in_b(k)[1], device_id_type=MESH)
        return carry

    lax.fori_loop(1, 32, greet_a, 0)
    lax.fori_loop(1, 8, greet_b, 0)
    for other in (next_tile, last_tile):
        pl.semaphore_signal(barrier, inc=1, device_id=other, device_id_type=MESH)
    pl.semaphore_wait(barrier, 40)

    to_next = pltpu.make_async_remote_copy(
        src_ref=noise_ref.at[pl.ds(24, 8)], dst_ref=extended.at[pl.ds(0, 8)], send_sem=halo_send.at[0],
        recv_sem=halo_recv.at[0], device_id=next_tile, device_id_type=MESH)
    to_last = pltpu.make_async_remote_copy(
        src_ref=noise_ref.at[pl.ds(0, 8)], dst_ref=extended.at[pl.ds(40, 8)], send_sem=halo_send.at[1],
        recv_sem=halo_recv.at[1], device_id=last_tile, device_id_type=MESH)

    @pl.when(s < 31)
    def _():
        to_next.start()

    @pl.when(s > 0)
    def _():
        to_last.start()

    own_load.wait()

    def send(rows, tile, send_sem, recv_sem, device):
        region = tiles.at[tile, rows]
        return pltpu.make_async_remote_copy(
            src_ref=region, dst_ref=region, send_sem=send_sem, recv_sem=recv_sem,
            device_id=device, device_id_type=MESH)

    classes = []
    start = 0
    for size, along_z_first, long_up in ((PA, True, True), (PB, True, False), (QA, False, True), (QB, False, False)):
        classes.append((pl.ds(start, size), along_z_first, long_up, False))
        start += size
    shared_base = start
    if RX:
        classes.append((pl.ds(pl.multiple_of(shared_base + x * RX, 16), RX), True, True, True))
    half = RX // 2

    def piece(owner, first, size):
        return pl.ds(pl.multiple_of(shared_base + owner * RX + first, 16), size)

    def placed(dy, i):
        dz = lax.rem(lax.div(i + 1, 2) * (2 * lax.rem(i, 2) - 1) + 8, 8)
        tile = lax.rem(y - dy + 4, 4) * 8 + lax.rem(z - dz + 8, 8)
        return tile, dy, dz

    def tile_of(n):
        part = lax.div(n, 8)
        middle = lax.rem(lax.div(part + 1, 2), 2)
        dy = middle * (1 + 2 * lax.rem(n, 2)) + 2 * lax.div(part, 3)
        return placed(dy, middle * lax.div(n - 8, 2) + (1 - middle) * lax.rem(n, 8))

    def across_of(n):
        col = lax.rem(n, 4)
        return placed(col + lax.div(col, 2) * (1 - 2 * lax.rem(col, 2)), lax.div(n, 4))

    def forward(n, chosen):
        for k in chosen:
            rows, along_z_first, long_up, shared = classes[k]
            tile, dy, dz = tile_of(n) if along_z_first else across_of(n)
            hi_z, hi_y = (4, 2) if long_up else (3, 1)

            @pl.when(n > 0)
            def _():
                send(rows, tile, tree_send.at[k], tree_recv.at[k, tile], sibling).wait_recv()

            go_zu = jnp.logical_or(dz == 0, jnp.logical_and(dz >= 1, dz < hi_z))
            go_zd = jnp.logical_or(dz == 0, dz > hi_z + 1)
            go_yu = jnp.logical_or(dy == 0, jnp.logical_and(dy >= 1, dy < hi_y))
            go_yd = jnp.logical_or(dy == 0, dy > hi_y + 1)
            if along_z_first:
                go_zu, go_zd = jnp.logical_and(go_zu, dy == 0), jnp.logical_and(go_zd, dy == 0)
            else:
                go_yu, go_yd = jnp.logical_and(go_yu, dz == 0), jnp.logical_and(go_yd, dz == 0)
            for go, device in ((go_zu, z_up), (go_zd, z_down), (go_yu, y_up), (go_yd, y_down)):
                @pl.when(go)
                def _():
                    send(rows, tile, tree_send.at[k], tree_recv.at[k, tile], device).start()
            if shared:
                @pl.when(n > 0)
                def _():
                    send(rows, tile, cross_send.at[0], cross_recv.at[0, tile], x_up).start()
                    send(rows, tile, cross_send.at[1], cross_recv.at[1, tile], x_down).start()

    def send_half(tile, device):
        region = halves.at[tile]
        return pltpu.make_async_remote_copy(
            src_ref=region, dst_ref=region, send_sem=half_send, recv_sem=half_recv.at[tile],
            device_id=device, device_id_type=MESH)

    def forward_half(n):
        tile, dy, dz = tile_of(n)

        @pl.when(n > 0)
        def _():
            send_half(tile, sibling).wait_recv()

        for go, device in ((jnp.logical_and(dy == 0, dz < 4), z_up),
                           (jnp.logical_and(dy == 0, jnp.logical_or(dz == 0, dz > 5)), z_down),
                           (dy < 2, y_up), (dy == 0, y_down)):
            @pl.when(go)
            def _():
                send_half(tile, device).start()

    def pass_on(n):
        tile, _, _ = tile_of(n)
        below, above = lax.rem(x + 3, 4), lax.rem(x + 1, 4)
        send(piece(below, 0, RX), tile, cross_send.at[0], cross_recv.at[0, tile], sibling).wait_recv()
        send(piece(below, 0, half), tile, cross_send.at[2], cross_recv.at[2, tile], x_up).start()
        send(piece(above, 0, RX), tile, cross_send.at[1], cross_recv.at[1, tile], sibling).wait_recv()
        send(piece(above, half, half), tile, cross_send.at[3], cross_recv.at[3, tile], x_down).start()

    def blocks_of(tile):
        return (tab_own[0, tile * 2], tab_own[0, tile * 2 + 1]), (tab_sib[0, tile * 2], tab_sib[0, tile * 2 + 1])

    def accumulate(tile, begin, end):
        (own_a, own_b), (sib_a, sib_b) = blocks_of(tile)
        total = accum[tile]
        for k in range(begin, end, 384):
            ks = pl.ds(k, min(384, end - k))
            lhs = jnp.concatenate(
                [own_f[own_a, :, ks], own_f[own_b, :, ks], sib_f[sib_a, :, ks], sib_f[sib_b, :, ks]], axis=0)
            total += jnp.dot(lhs, tiles[tile, ks, :], preferred_element_type=jnp.float32)
        accum[tile] = total

    def finish_tile(tile, carry):
        total = (accum[tile] * JAC_SCALE).astype(jnp.bfloat16)
        rows = pl.ds(pl.multiple_of(tile * 64, 64), 64)
        jac[c, rows, :] = total[:64]
        jac_out[rows, :] = total[64:]
        return carry

    def multiply(n):
        tile, _, _ = tile_of(n)
        if RX:
            far = lax.rem(x + 2, 4)

            @pl.when(n > 0)
            def _():
                send(piece(far, 0, half), tile, cross_send.at[2], cross_recv.at[2, tile], sibling).wait_recv()
                send(piece(far, half, half), tile, cross_send.at[3], cross_recv.at[3, tile], sibling).wait_recv()
        (own_a, own_b), _ = blocks_of(tile)
        accumulate(tile, 0, PA + PB)
        accumulate(tile, PA + PB + QA + QB, 4096)
        values = halves[tile].astype(jnp.float32)
        seen_a = jnp.zeros((32, 128), jnp.float32)
        seen_b = jnp.zeros((32, 128), jnp.float32)
        for k in range(32):
            ks = pl.ds(k * 128, 128)
            value = values[k:k + 1, :]
            seen_a += own_f[own_a, :, ks].astype(jnp.float32) * value
            seen_b += own_f[own_b, :, ks].astype(jnp.float32) * value
        rows = pl.ds(pl.multiple_of(tile * 64, 64), 64)
        seen = lax.dot_general(jnp.ones((8, 128), jnp.float32), jnp.concatenate([seen_a, seen_b], axis=0),
                               (((1,), (1,)), ((), ())), precision=HIGHEST, preferred_element_type=jnp.float32)
        accs[pl.ds(tile, 1), 0:64] = seen[0:1, :]
        lane = lax.broadcasted_iota(jnp.int32, (32, 128), 1)
        gaps[rows, :] = jnp.concatenate(
            [jnp.where(lane == own_a, sound_t[...], 0.0) - seen_a,
             jnp.where(lane == own_b, sound_t[...], 0.0) - seen_b], axis=0)

    forward(0, (4, 0, 2))
    source, even, odd = slot_tables(target_ref[...])
    tab_mine[...] = source
    tab_load = pltpu.make_async_copy(tab_mine, tab_own, load_sem.at[2])
    tab_load.start()
    tab_swap = pltpu.make_async_remote_copy(
        src_ref=tab_mine, dst_ref=tab_v, send_sem=pair_send.at[0], recv_sem=pair_recv.at[0],
        device_id=sibling, device_id_type=MESH)
    tab_swap.start()
    square[...] = jnp.zeros(square.shape, jnp.float32)
    square[0:32, 0:32] = sound_ref[...].astype(jnp.float32)
    sound_t[...] = square[...].T[0:32, :]
    fp_swap = pltpu.make_async_remote_copy(
        src_ref=fp_ref.at[0], dst_ref=sib_f.at[pl.ds(0, count)], send_sem=pair_send.at[1],
        recv_sem=pair_recv.at[1], device_id=sibling, device_id_type=MESH)
    fp_swap.start()
    own_f[count] = jnp.zeros(own_f.shape[1:], own_f.dtype)
    sib_f[count] = jnp.zeros(sib_f.shape[1:], sib_f.dtype)
    columns, (band_even, band_up, band_down) = smoothing_matrices()
    extended[8:40, :] = noise_ref[...]

    @pl.when(s > 0)
    def _():
        to_next.wait_recv()

    @pl.when(s == 0)
    def _():
        extended[0:8, :] = jnp.zeros((8, 128), jnp.float32)

    @pl.when(s < 31)
    def _():
        to_last.wait_recv()

    @pl.when(s == 31)
    def _():
        extended[40:48, :] = jnp.zeros((8, 128), jnp.float32)

    def exact(p, q):
        return jnp.dot(p, q, precision=HIGHEST, preferred_element_type=jnp.float32)

    mixed = exact(extended[...], columns)
    swapped = jnp.concatenate([mixed[:, 64:], mixed[:, :64]], axis=1)
    lane = lax.broadcasted_iota(jnp.int32, (32, 128), 1)
    smooth = exact(band_even, mixed) + jnp.where(
        lane < 64, exact(band_up, swapped), exact(band_down, swapped))
    proposal = KEEP * flux_ref[...] + BETA * prior_ref[...] * smooth
    proposal_ref[...] = proposal
    halves[s] = proposal.astype(jnp.bfloat16)
    forward_half(0)
    tab_swap.wait()
    sib_load = pltpu.make_async_copy(tab_v, tab_sib, load_sem.at[3])
    sib_load.start()
    tab_load.wait()
    sib_load.wait()

    def cross_item(m):
        @pl.when(m < 32)
        def _():
            forward(m, (4,))

        @pl.when(m > LAG_CROSS)
        def _():
            pass_on(m - LAG_CROSS)

    def early_item(m, carry):
        cross_item(m)
        return carry

    def step(n, carry):
        @pl.when(n < 32)
        def _():
            forward(n, (2, 3))

        @pl.when(n + AHEAD < 32 + LAG_CROSS)
        def _():
            cross_item(n + AHEAD)

        @pl.when(n < 32)
        def _():
            forward(n, (0, 1))
            forward_half(n)

        @pl.when(n == LAG_WORK)
        def _():
            fp_load.wait()
            fp_swap.wait()

        @pl.when(n >= LAG_WORK)
        def _():
            multiply(n - LAG_WORK)
            accumulate(across_of(n - LAG_WORK)[0], PA + PB, PA + PB + QA + QB)
        return carry

    lax.fori_loop(1, 2, early_item, 0)
    forward(0, (3,))
    lax.fori_loop(2, 6, early_item, 0)
    forward(0, (1,))
    lax.fori_loop(6, 12, early_item, 0)
    accum[...] = jnp.zeros(accum.shape, jnp.float32)
    lax.fori_loop(1, 32 + LAG_WORK, step, 0)
    lax.fori_loop(0, 32, finish_tile, 0)
    whole = pltpu.make_async_remote_copy(
        src_ref=jac_out, dst_ref=jac.at[c], send_sem=jac_send, recv_sem=jac_recv,
        device_id=sibling, device_id_type=MESH)
    whole.start()
    mis = lax.dot_general(jnp.ones((8, 128), jnp.float32), gaps[...], (((1,), (1,)), ((), ())),
                          precision=HIGHEST, preferred_element_type=jnp.float32)

    for k, (rows, _, _, _) in enumerate(classes):
        region = tiles.at[pl.ds(0, 31), rows]
        pltpu.make_async_copy(region, region, tree_send.at[k]).wait()
    if RX:
        for k, size in enumerate((RX, RX, half, half)):
            region = tiles.at[pl.ds(0, 31), pl.ds(0, size)]
            pltpu.make_async_copy(region, region, cross_send.at[k]).wait()
    whole.wait()
    region = halves.at[pl.ds(0, 31)]
    pltpu.make_async_copy(region, region, half_send).wait()

    @pl.when(s < 31)
    def _():
        to_next.wait_send()

    @pl.when(s > 0)
    def _():
        to_last.wait_send()

    low, high = jac[0], jac[1]

    def gram(a, b):
        return lax.dot_general(a, b, (((0,), (0,)), ((), ())), preferred_element_type=jnp.float32)

    upper_rows = gram(low, jnp.concatenate([low, high], axis=1))
    aug[0:128, :] = upper_rows[:, 0:128]
    aug[128:256, :] = upper_rows[:, 128:256]
    aug[256:384, :] = gram(high, high)
    mis_a = mis.astype(jnp.bfloat16)
    rest = mis - mis_a.astype(jnp.float32)
    mis_b = rest.astype(jnp.bfloat16)
    mis_c = (rest - mis_b.astype(jnp.float32)).astype(jnp.bfloat16)
    aug[384:, :] = jnp.zeros((128, 128), jnp.float32)
    for k, side in enumerate((low, high)):
        part = sum(jnp.dot(m, side, preferred_element_type=jnp.float32) for m in (mis_c, mis_b, mis_a))
        aug[384 + 8 * k:392 + 8 * k, :] = part

    def rows(index):
        return pl.ds(pl.multiple_of(index * 16, 16), 16)

    def scatter(k, carry):
        other, device = in_a(k)
        pltpu.make_async_remote_copy(
            src_ref=aug.at[rows(other)], dst_ref=parts.at[k - 1], send_sem=send_a, recv_sem=recv_a,
            device_id=device, device_id_type=MESH).start()
        return carry

    lax.fori_loop(1, 32, scatter, 0)

    def settle(region, send_sem, recv_sem):
        pltpu.make_async_copy(region, region, send_sem).wait()
        pltpu.make_async_copy(region, region, recv_sem).wait()

    predicted_ref[...] = exact(even, accs[:, 0:32]) + exact(odd, accs[:, 32:64])
    settle(parts, send_a, recv_a)
    own = aug[rows(a), :]
    for k in range(31):
        own = own + parts[k]
    sums[b] = own

    def exchange(k, carry):
        _, device = in_b(k)
        pltpu.make_async_remote_copy(
            src_ref=sums.at[b], dst_ref=sums.at[b], send_sem=send_b, recv_sem=recv_b,
            device_id=device, device_id_type=MESH).start()
        return carry

    lax.fori_loop(1, 8, exchange, 0)
    settle(parts.at[pl.ds(0, 7)], send_b, recv_b)
    total = sums[0]
    for k in range(1, 8):
        total = total + sums[k]
    full[rows(a), :] = total

    def spread(k, carry):
        _, device = in_a(k)
        pltpu.make_async_remote_copy(
            src_ref=full.at[rows(a)], dst_ref=full.at[rows(a)], send_sem=send_c, recv_sem=recv_c,
            device_id=device, device_id_type=MESH).start()
        return carry

    lax.fori_loop(1, 32, spread, 0)
    settle(parts, send_c, recv_c)


def factor_kernel(full, proposal_in, predicted_in, proposal_ref, predicted_ref, u_ref, v_ref, work, solved):
    proposal_ref[...] = proposal_in[...]
    predicted_ref[...] = predicted_in[...]
    square = (128, 128)
    eye = (lax.broadcasted_iota(jnp.int32, square, 0) == lax.broadcasted_iota(jnp.int32, square, 1))
    eye = eye.astype(jnp.float32)
    rhs = full[384:512, :].T
    work[0:128, 0:128] = full[0:128, :] + eye
    work[0:128, 128:256] = full[128:256, :]
    work[128:256, 128:256] = full[256:384, :] + eye
    work[0:128, 256:384] = rhs
    work[128:256, 256:384] = jnp.concatenate([rhs[:, 8:], rhs[:, :8]], axis=1)
    factor_rows(work, u_ref, solved)
    v_ref[:, 0:128] = solved[0:128, :].T[0:1, :]
    v_ref[:, 128:256] = solved[128:256, :].T[0:1, :]


def whole_step(flux, noise, prior, target, sound, footprints, basis):
    vm = pl.BlockSpec(memory_space=pltpu.VMEM)
    hbm = pl.BlockSpec(memory_space=pl.ANY)
    dma = pltpu.SemaphoreType.DMA
    f32, bf16, i32 = jnp.float32, jnp.bfloat16, jnp.int32
    shapes = (jax.ShapeDtypeStruct((32, 128), f32), jax.ShapeDtypeStruct((32, 32), f32))
    proposal, predicted, summed = pl.pallas_call(
        step_kernel,
        out_shape=shapes + (jax.ShapeDtypeStruct((512, 128), f32),),
        in_specs=[vm, vm, vm, vm, vm, hbm, hbm],
        out_specs=(vm, vm, vm),
        scratch_shapes=[
            pltpu.VMEM((33, 32, 4096), bf16), pltpu.VMEM((33, 32, 4096), bf16),
            pltpu.VMEM((32, 4096, 128), bf16), pltpu.VMEM((32, 32, 128), bf16),
            pltpu.VMEM((2, 2048, 128), bf16), pltpu.VMEM((2048, 128), bf16),
            pltpu.VMEM((32, 128), f32), pltpu.VMEM((2048, 128), f32), pltpu.VMEM((48, 128), f32),
            pltpu.VMEM((128, 128), f32), pltpu.VMEM((32, 128), f32),
            pltpu.VMEM((1, 128), i32), pltpu.VMEM((1, 128), i32), pltpu.SMEM((1, 128), i32), pltpu.SMEM((1, 128), i32),
            pltpu.VMEM((512, 128), f32), pltpu.VMEM((31, 16, 128), f32), pltpu.VMEM((8, 16, 128), f32), pltpu.VMEM((32, 128, 128), f32),
            dma((4,)), dma((2,)), dma((2,)), dma((5, 32)), dma((4, 32)), dma((5,)), dma((4,)),
            dma, dma, dma, dma((32,)), dma((2,)), dma((2,)),
            dma, dma, dma, dma, dma, dma,
        ],
        compiler_params=pltpu.CompilerParams(
            collective_id=0, has_side_effects=True, vmem_limit_bytes=60 * 1024 * 1024),
        name="assimilate",
    )(flux, noise, prior, target, sound, footprints, basis)
    return pl.pallas_call(
        factor_kernel,
        out_shape=shapes + (jax.ShapeDtypeStruct((256, 256), f32), jax.ShapeDtypeStruct((1, 256), f32)),
        in_specs=[vm, vm, vm],
        out_specs=(vm, vm, vm, vm),
        scratch_shapes=[pltpu.VMEM((256, 384), f32), pltpu.VMEM((256, 128), f32)],
        name="factor",
    )(summed, proposal, predicted)


def per_device(flux, noise, prior_scale, footprints, soundings, targets, basis):
    proposal, predicted, factor_up, rhs_value = whole_step(
        flux.reshape(32, 128), noise.reshape(32, 128), prior_scale.reshape(32, 128),
        targets.reshape(1, 32), soundings.reshape(32, 32), footprints, basis)
    return (proposal.reshape(1, 4096), predicted[None], factor_up, rhs_value.reshape(256))


def solution(mesh):
    return jax.shard_map(
        per_device,
        mesh=mesh,
        in_specs=(
            P("tm", "space"),
            P("tm", "space"),
            P("space"),
            P("tm", "space", None, None),
            P("tm", "space", None),
            P("tm", "space", None),
            P("space", None),
        ),
        out_specs=(P("tm", "space"), P("tm", "space", None), P(), P()),
        check_vma=False,
    )
```
